32 devices in a mesh: leaf: 8 (over z, y), sub: 4 (over x, core).
Axes of the slice: x: 2, y: 2, z: 4, core: 2. Of those that a mesh axis runs over, the one named last changes fastest.
Arguments:
- points: bfloat16 [512, 64, 256], P(('leaf', 'sub')), may hold values from -6 to 6
- probe_bits: int32 [512, 16, 256], P(('leaf', 'sub')), may hold values from 0 to 1
- leaf_skel: int32 [512, 128], P(('leaf', 'sub')), may hold values from 0 to 255, as said below
- leaf_basis: bfloat16 [512, 128, 256], P(('leaf', 'sub')), may hold values from -0.4375 to 0.4375
- device_skel: int32 [32, 128], P(('leaf', 'sub')), may hold values from 0 to 2047, as said below
- device_basis: bfloat16 [32, 128, 2048], P(('leaf', 'sub')), may hold values from -0.25 to 0.25
- subtree_skel: int32 [8, 128], P('leaf'), may hold values from 0 to 511, as said below
- subtree_basis: bfloat16 [8, 128, 512], P('leaf'), may hold values from -0.375 to 0.375
- upper_skel: int32 [8, 2, 128], P('leaf'), may hold values from 0 to 255, as said below
- upper_basis: bfloat16 [8, 2, 128, 256], P('leaf'), as said below
- near_pairs: int32 [32, 80, 2], P(('leaf', 'sub')), may hold values from 0 to 63, as said below
- near_count: int32 [32], P(('leaf', 'sub')), may hold values from 1 to 80, 1024 in all
- far_pairs: int32 [32, 96, 2], P(('leaf', 'sub')), may hold values from 0 to 63, as said below
Outputs:
- product: float32 [512, 16, 256], P(('leaf', 'sub'))
The draws below stay inside these ranges and needn't reach their ends.
Inputs may be any that keep to these rules, and one draw needn't show every extreme that they name: `leaf_skel`: each row names 128 different points of its leaf. `device_skel`: each row names 128 different columns. `subtree_skel`: each row names 128 different columns. `upper_skel`: each row names 128 different columns; entries [g, t-1] are equal for all subtrees g under one node of level t. `upper_basis`: entries [g, t-1] are equal for all subtrees g under one node of level t. `near_pairs`: entry 0 of a row is a leaf of the device (0 to 15), entry 1 a leaf of its subtree numbered 0 to 63 in the subtree, never the first leaf itself; the rows of one device are different pairs. `near_count`: some device has exactly 80 pairs. `far_pairs`: as for near_pairs; every row is used.
All inputs are finite; a program needn't handle non-finite values.
Results may differ from the reference program's by a relative error of at most 0.013.
Values may be sent and summed in bfloat16 or wider, within the bound.
No kernel may reach another device: no remote copies, remote signals or barrier semaphores. Data moves between devices by JAX's collectives and lax.ppermute only.
A program may use at most 128 MiB of HBM per device.

```python
import math
import jax
import jax.numpy as jnp
import numpy as np
from jax import lax

FEATURES = 64
LEAF_SIZE = 256
SKELETON = 128
PROBES = 16
LEAF_DEV = 16
NEAR_CAP = 80
FAR_DEV = 96
SUB_LEAVES = 64
LEAVES = 512
LEVELS = 3
N_LEAF = 8
N_SUB = 4
DEVICES = 32


def distinct_rows(key, rows, pool_size, take_count):
    row_keys = jax.random.split(key, rows)
    picked = jax.vmap(lambda row_key: jax.random.permutation(row_key, pool_size)[:take_count])(row_keys)
    return picked.astype(jnp.int32)


def pair_lists(key, count):
    span = LEAF_DEV * N_SUB - 1
    picked = distinct_rows(key, DEVICES, LEAF_DEV * span, count)
    local_leaf = picked // span
    other_leaf = picked % span
    own_index = (jnp.arange(DEVICES, dtype=jnp.int32) % N_SUB)[:, None] * LEAF_DEV + local_leaf
    partner = other_leaf + (other_leaf >= own_index).astype(jnp.int32)
    return jnp.stack([local_leaf, partner], axis=-1).astype(jnp.int32)


def draw_leaf_skel(key, part):
    return distinct_rows(jax.random.fold_in(key, 11), LEAVES, LEAF_SIZE, SKELETON)


def draw_device_skel(key, part):
    return distinct_rows(jax.random.fold_in(key, 13), DEVICES, LEAF_DEV * SKELETON, SKELETON)


def draw_subtree_skel(key, part):
    return distinct_rows(jax.random.fold_in(key, 17), N_LEAF, N_SUB * SKELETON, SKELETON)


def draw_upper_skel(key, part):
    stacked = []
    for height in range(1, LEVELS):
        node_rows = distinct_rows(jax.random.fold_in(key, 41 + height), N_LEAF >> height, 2 * SKELETON, SKELETON)
        stacked.append(jnp.repeat(node_rows, 2 ** height, axis=0))
    return jnp.stack(stacked, axis=1).astype(jnp.int32)


def draw_upper_basis(key, part):
    stacked = []
    for height in range(1, LEVELS):
        values = jax.random.normal(jax.random.fold_in(key, 71 + height), (N_LEAF >> height, SKELETON, 2 * SKELETON), jnp.float32)
        values = jnp.clip(values, -6.0, 6.0) * (1.5 * SKELETON) ** (-0.5)
        stacked.append(jnp.repeat(values, 2 ** height, axis=0))
    return jnp.stack(stacked, axis=1).astype(jnp.bfloat16)


def draw_near_pairs(key, part):
    return pair_lists(jax.random.fold_in(key, 23), NEAR_CAP)


def draw_far_pairs(key, part):
    return pair_lists(jax.random.fold_in(key, 29), FAR_DEV)


def touch_ends(result, key, low, high):
    longest = result.shape.index(max(result.shape))
    spots = []
    for shift in (0, 1):
        where = [jax.random.randint(jax.random.fold_in(key, axis), (), 0, length) for axis, length in enumerate(result.shape)]
        where[longest] = (where[longest] + shift) % result.shape[longest]
        spots.append(tuple(where))
    return result.at[spots[0]].set(low).at[spots[1]].set(high)


def level_of(key, shape, shards, low, top_value):
    loudness = 1.0
    for dim, blocks in shards:
        heights = jax.random.uniform(jax.random.fold_in(jax.random.fold_in(key, 6), dim), (blocks,), jnp.float32, low / len(shards), top_value / len(shards))
        loudness = loudness * jnp.repeat(jnp.exp(heights), shape[dim] // blocks).reshape((-1,) + (1,) * (len(shape) - 1 - dim))
    return loudness


def length_profile(number_of, total, most, lean):
    weights = [(1 << 20) // math.isqrt(rank ** lean) + 1 for rank in range(2, number_of + 1)]
    spare, given = total - most - (number_of - 1), [1] * (number_of - 1)
    while spare > 0:
        free = [i for i in range(number_of - 1) if given[i] < most]
        pool, remaining = sum([weights[i] for i in free]), spare
        for i in free:
            addition = min(most - given[i], max(1, remaining * weights[i] // pool), spare)
            given[i] = given[i] + addition
            spare = spare - addition
    return np.array([most] + given)


def uneven_parts(key, number_of, total, limit, lean):
    if number_of == 2:
        one = jax.random.randint(key, (), max(1, total - limit), min(limit, total - 1) + 1)
        return jnp.stack([one, total - one])
    tallies = jnp.asarray(length_profile(number_of, total, limit, lean), jnp.int32)
    couples = (number_of - 1) // 2
    source_of, receiver = tallies[1:1 + 2 * couples:2], tallies[2:2 + 2 * couples:2]
    room = jnp.minimum(source_of - 1, limit - receiver)
    shifted = jax.random.randint(jax.random.fold_in(key, 1), (couples,), 0, 1 << 20) % (room + 1)
    tallies = tallies.at[1:1 + 2 * couples:2].set(source_of - shifted).at[2:2 + 2 * couples:2].set(receiver + shifted)
    return tallies[jax.random.permutation(jax.random.fold_in(key, 2), number_of)]


def bell_draw(stream_key, extent, deviation, most, pieces=(), kind=jnp.bfloat16):
    values = deviation * jax.random.normal(stream_key, extent, jnp.float32)
    if pieces:
        values = values * level_of(stream_key, extent, pieces, -0.22, 0.18)
    return jnp.clip(values, -most, most).astype(kind)


def setup_inputs(seed: int = 0) -> dict:
    streams_of = jax.random.split(jax.random.key(seed), 14)
    return {
        "points": bell_draw(streams_of[0], (LEAVES, FEATURES, LEAF_SIZE), 1.0, 6.0, ((0, 32),)),
        "probe_bits": touch_ends(jax.random.randint(streams_of[1], (LEAVES, PROBES, LEAF_SIZE), 0, 2), jax.random.fold_in(streams_of[1], 1), 0, 1).astype(jnp.int32),
        "leaf_skel": draw_leaf_skel(jax.random.fold_in(streams_of[13], 71), 0),
        "leaf_basis": bell_draw(streams_of[3], (LEAVES, SKELETON, LEAF_SIZE), (SKELETON + SKELETON // 2) ** -0.5, 0.4375, ((0, 32),)),
        "device_skel": draw_device_skel(jax.random.fold_in(streams_of[13], 71), 0),
        "device_basis": bell_draw(streams_of[5], (DEVICES, SKELETON, LEAF_DEV * SKELETON), (SKELETON * (1 + LEAF_DEV // 4)) ** -0.5, 0.25, ((0, 32),)),
        "subtree_skel": draw_subtree_skel(jax.random.fold_in(streams_of[13], 71), 0),
        "subtree_basis": bell_draw(streams_of[7], (N_LEAF, SKELETON, N_SUB * SKELETON), (SKELETON * max(1, N_SUB // 2)) ** -0.5, 0.375, ((0, 8),)),
        "upper_skel": draw_upper_skel(jax.random.fold_in(streams_of[13], 71), 0),
        "upper_basis": draw_upper_basis(jax.random.fold_in(streams_of[13], 71), 0),
        "near_pairs": draw_near_pairs(jax.random.fold_in(streams_of[13], 71), 0),
        "near_count": uneven_parts(streams_of[11], DEVICES, DEVICES * NEAR_CAP * 2 // 5, NEAR_CAP, 2).astype(jnp.int32),
        "far_pairs": draw_far_pairs(jax.random.fold_in(streams_of[13], 71), 0),
    }


def kernel_tile(first_set, second_set):
    first_wide = first_set.astype(jnp.float32)
    second_wide = second_set.astype(jnp.float32)
    cross_terms = jnp.einsum('...da,...db->...ab', first_wide, second_wide)
    first_norm = jnp.sum(first_wide * first_wide, axis=-2)
    second_norm = jnp.sum(second_wide * second_wide, axis=-2)
    distance = first_norm[..., :, None] + second_norm[..., None, :] - 2.0 * cross_terms
    return jnp.exp(-distance / FEATURES).astype(jnp.bfloat16)


def joined(parts):
    shape_now = parts.shape
    moved = jnp.transpose(parts, (0, 2, 1, 3))
    return moved.reshape(shape_now[0], shape_now[2], shape_now[1] * shape_now[3])


def apply_up(weights, bases):
    return jnp.einsum('npc,nrc->npr', weights.astype(jnp.float32), bases.astype(jnp.float32)).astype(jnp.bfloat16)


def apply_down(potential, bases):
    rounded = potential.astype(jnp.bfloat16).astype(jnp.float32)
    return jnp.einsum('npr,nrc->npc', rounded, bases.astype(jnp.float32))


def select_columns(coords, skeleton):
    return jnp.take_along_axis(coords, skeleton[:, None, :].astype(jnp.int32), axis=2)


def device_terms(device_data):
    leaf_points, leaf_bits, leaf_skeleton, leaf_bases, device_skeleton, device_bases = device_data
    sign_values = (2 * leaf_bits - 1).astype(jnp.bfloat16)
    coords = select_columns(leaf_points, leaf_skeleton)
    weights = jnp.einsum('lpm,lrm->lpr', sign_values.astype(jnp.float32), leaf_bases.astype(jnp.float32)).astype(jnp.bfloat16)
    joined_weights = jnp.transpose(weights, (1, 0, 2)).reshape(PROBES, LEAF_DEV * SKELETON)
    joined_coords = jnp.transpose(coords, (1, 0, 2)).reshape(FEATURES, LEAF_DEV * SKELETON)
    node_weights = jnp.einsum('pc,rc->pr', joined_weights.astype(jnp.float32), device_bases.astype(jnp.float32)).astype(jnp.bfloat16)
    node_coords = jnp.take(joined_coords, device_skeleton.astype(jnp.int32), axis=1)
    return coords, weights, node_coords, node_weights


def subtree_terms(subtree_data):
    leaf_points, leaf_bits, leaf_bases, coords, weights, leaf_pot, near_list, counts, far_list = subtree_data
    sign_values = (2 * leaf_bits - 1).astype(jnp.bfloat16)
    signs_wide = sign_values.astype(jnp.float32)
    self_block = kernel_tile(leaf_points, leaf_points).astype(jnp.float32)
    result_sum = jnp.einsum('lpm,lmn->lpn', signs_wide, self_block)
    per_block = min(16, NEAR_CAP)
    for owner_dev in range(N_SUB):
        first_all = (owner_dev * LEAF_DEV + near_list[owner_dev, :, 0]).astype(jnp.int32)
        second_all = near_list[owner_dev, :, 1].astype(jnp.int32)
        count_now = counts[owner_dev]

        def near_step(counter, partial_value, first_all=first_all, second_all=second_all, count_now=count_now):
            slot_ids = counter * per_block + jnp.arange(per_block, dtype=jnp.int32)
            live_mask = (slot_ids < count_now).astype(jnp.float32)[:, None, None]
            slot_ids = jnp.minimum(slot_ids, NEAR_CAP - 1)
            first_leaf = first_all[slot_ids]
            second_leaf = second_all[slot_ids]
            kernel_block = kernel_tile(leaf_points[second_leaf], leaf_points[first_leaf]).astype(jnp.float32)
            to_first = jnp.einsum('fpm,fmn->fpn', signs_wide[second_leaf], kernel_block) * live_mask
            to_second = jnp.einsum('fpn,fmn->fpm', signs_wide[first_leaf], kernel_block) * live_mask
            return partial_value.at[first_leaf].add(to_first).at[second_leaf].add(to_second)

        rounds = (count_now + per_block - 1) // per_block
        result_sum = lax.fori_loop(0, rounds, near_step, result_sum)
    owner_base = jnp.arange(N_SUB, dtype=jnp.int32)[:, None] * LEAF_DEV
    far_first = (owner_base + far_list[:, :, 0]).reshape(-1).astype(jnp.int32)
    far_second = far_list[:, :, 1].reshape(-1).astype(jnp.int32)
    far_block = kernel_tile(coords[far_second], coords[far_first]).astype(jnp.float32)
    to_first_far = jnp.einsum('fpb,fba->fpa', weights[far_second].astype(jnp.float32), far_block).astype(jnp.bfloat16).astype(jnp.float32)
    to_second_far = jnp.einsum('fpa,fba->fpb', weights[far_first].astype(jnp.float32), far_block).astype(jnp.bfloat16).astype(jnp.float32)
    gathered = jnp.zeros((SUB_LEAVES, PROBES, SKELETON), jnp.float32)
    gathered = gathered.at[far_first].add(to_first_far).at[far_second].add(to_second_far)
    bases_wide = leaf_bases.astype(jnp.float32)
    result_sum = result_sum + jnp.einsum('lpr,lrm->lpm', leaf_pot.astype(jnp.bfloat16).astype(jnp.float32), bases_wide)
    result_sum = result_sum + jnp.einsum('lpr,lrm->lpm', gathered, bases_wide, precision=lax.Precision.HIGHEST)
    return result_sum


def reference(points, probe_bits, leaf_skel, leaf_basis, device_skel, device_basis, subtree_skel, subtree_basis, upper_skel, upper_basis, near_pairs, near_count, far_pairs):
    device_data = (points.reshape(DEVICES, LEAF_DEV, FEATURES, LEAF_SIZE), probe_bits.reshape(DEVICES, LEAF_DEV, PROBES, LEAF_SIZE), leaf_skel.reshape(DEVICES, LEAF_DEV, SKELETON), leaf_basis.reshape(DEVICES, LEAF_DEV, SKELETON, LEAF_SIZE), device_skel, device_basis)
    leaf_coords, leaf_weights, device_coords, device_weights = lax.map(device_terms, device_data)
    node_weights = apply_up(joined(device_weights.reshape(N_LEAF, N_SUB, PROBES, SKELETON)), subtree_basis)
    node_coords = select_columns(joined(device_coords.reshape(N_LEAF, N_SUB, FEATURES, SKELETON)), subtree_skel)
    far_terms = []
    for height in range(1, LEVELS + 1):
        left_coords, right_coords = node_coords[0::2], node_coords[1::2]
        left_weights, right_weights = node_weights[0::2], node_weights[1::2]
        kernel_block = kernel_tile(right_coords, left_coords).astype(jnp.float32)
        to_left = jnp.einsum('kpr,krl->kpl', right_weights.astype(jnp.float32), kernel_block)
        to_right = jnp.einsum('kpl,krl->kpr', left_weights.astype(jnp.float32), kernel_block)
        far_terms.append((to_left, to_right))
        if height < LEVELS:
            group_ids = jnp.arange(N_LEAF >> height, dtype=jnp.int32) * (2 ** height)
            node_weights = apply_up(jnp.concatenate([left_weights, right_weights], axis=2), upper_basis[group_ids, height - 1])
            node_coords = select_columns(jnp.concatenate([left_coords, right_coords], axis=2), upper_skel[group_ids, height - 1])
    potential = jnp.zeros((1, PROBES, SKELETON), jnp.float32)
    for height in range(LEVELS, 0, -1):
        to_left, to_right = far_terms[height - 1]
        if height < LEVELS:
            group_ids = jnp.arange(N_LEAF >> height, dtype=jnp.int32) * (2 ** height)
            spread = apply_down(potential, upper_basis[group_ids, height - 1])
            to_left = to_left + spread[:, :, :SKELETON]
            to_right = to_right + spread[:, :, SKELETON:]
        potential = jnp.stack([to_left, to_right], axis=1).reshape(-1, PROBES, SKELETON)
    sub_spread = apply_down(potential, subtree_basis)
    device_potential = jnp.transpose(sub_spread.reshape(N_LEAF, PROBES, N_SUB, SKELETON), (0, 2, 1, 3)).reshape(DEVICES, PROBES, SKELETON)
    dev_spread = apply_down(device_potential, device_basis)
    leaf_potential = jnp.transpose(dev_spread.reshape(DEVICES, PROBES, LEAF_DEV, SKELETON), (0, 2, 1, 3))
    subtree_data = (points.reshape(N_LEAF, SUB_LEAVES, FEATURES, LEAF_SIZE), probe_bits.reshape(N_LEAF, SUB_LEAVES, PROBES, LEAF_SIZE), leaf_basis.reshape(N_LEAF, SUB_LEAVES, SKELETON, LEAF_SIZE), leaf_coords.reshape(N_LEAF, SUB_LEAVES, FEATURES, SKELETON), leaf_weights.reshape(N_LEAF, SUB_LEAVES, PROBES, SKELETON), leaf_potential.reshape(N_LEAF, SUB_LEAVES, PROBES, SKELETON), near_pairs.reshape(N_LEAF, N_SUB, NEAR_CAP, 2), near_count.reshape(N_LEAF, N_SUB), far_pairs.reshape(N_LEAF, N_SUB, FAR_DEV, 2))
    results = lax.map(subtree_terms, subtree_data)
    return results.reshape(LEAVES, PROBES, LEAF_SIZE)
```

```python
import functools

import jax
import jax.numpy as jnp
from jax import lax
from jax.experimental import pallas as pl
from jax.experimental.pallas import tpu as pltpu
from jax.sharding import PartitionSpec as P

BF16 = jnp.bfloat16
F32 = jnp.float32
AUG = 16
NEAR_STEP = 16
FAR_STEP = 32
LIST_ROWS = 16
VMEM = pl.BlockSpec(memory_space=pltpu.VMEM)
SMEM = pl.BlockSpec(memory_space=pltpu.SMEM)
ANY = pl.BlockSpec(memory_space=pl.ANY)
VMEM_LIMIT = 56 << 20


def flipped(block, axis, bits):
    count = lax.axis_size(axis)
    return lax.ppermute(block, axis, [(low, low ^ bits) for low in range(count)])


def dot(left, right, left_dim, right_dim):
    return lax.dot_general(
        left, right, (((left_dim,), (right_dim,)), ((), ())), preferred_element_type=F32
    )


def one_hot(columns, rows, start=0):
    spots = lax.broadcasted_iota(jnp.int32, (rows, columns.shape[1]), 0) + start
    return jnp.where(spots == columns, 1.0, 0.0).astype(BF16)


def norm_parts(coords):
    wide = coords.astype(F32)
    norm = jnp.sum(wide * wide, axis=0, keepdims=True) * (-1.0 / coords.shape[0])
    high = norm.astype(BF16).astype(F32)
    rest = norm - high
    middle = rest.astype(BF16).astype(F32)
    return high, middle, rest - middle


def aug_rows(parts, width, norm_first):
    row = lax.broadcasted_iota(jnp.int32, (AUG, width), 0)
    start, ones = (0, 3) if norm_first else (3, 0)
    block = jnp.where((row >= ones) & (row < ones + 3), 1.0, 0.0)
    for index, part in enumerate(parts):
        block = jnp.where(row == start + index, part, block)
    return block.astype(BF16)


def with_norms(coords, norm_first):
    rows = aug_rows(norm_parts(coords), coords.shape[1], norm_first)
    scaled = (coords.astype(F32) * (2.0 / coords.shape[0])).astype(BF16) if norm_first else coords
    return jnp.concatenate([scaled, rows], axis=0)


def tile(left, right, left_dim, right_dim):
    return jnp.exp(dot(left, right, left_dim, right_dim)).astype(BF16)


def list_row(pairs, row, width):
    count = pairs.shape[0]
    pick = lax.broadcasted_iota(jnp.int32, (8, 2), 0) == lax.broadcasted_iota(
        jnp.int32, (8, 2), 1
    ) + row
    rows = dot(jnp.where(pick, 1.0, 0.0).astype(BF16), pairs.astype(F32).astype(BF16), 1, 1)
    if count == width:
        return rows
    return jnp.concatenate([rows, jnp.zeros((8, width - count), F32)], axis=1)


def prep_kernel(
    points, bits, leaf_skel, leaf_basis, dev_skel, dev_basis, near, near_count, far, q1, q2
):
    leaves, features, size = points.shape
    probes = bits.shape[1]
    skeleton = leaf_skel.shape[1]
    node_weights = jnp.zeros((probes, skeleton), F32)
    node_coords = jnp.zeros((features, skeleton), F32)
    for leaf in range(leaves):
        span = slice(leaf * skeleton, (leaf + 1) * skeleton)
        signs = (2 * bits[leaf] - 1).astype(F32).astype(BF16)
        q2[leaf, :, :size] = signs
        weights = dot(signs, leaf_basis[leaf], 1, 1).astype(BF16)
        q2[leaf, :, size:] = weights
        node_weights += dot(weights, dev_basis[0, :, span], 1, 1)
        coords = dot(points[leaf], one_hot(leaf_skel[leaf : leaf + 1, :], size), 1, 0).astype(BF16)
        node_coords += dot(coords, one_hot(dev_skel[...], skeleton, leaf * skeleton), 1, 0)
    q1[:features] = node_coords.astype(BF16)
    q1[features : features + probes] = node_weights.astype(BF16)
    lists = list_row(near[0], 0, skeleton) + list_row(far[0], 2, skeleton)
    row = lax.broadcasted_iota(jnp.int32, lists.shape, 0)
    lists = jnp.where(row == 4, near_count[0].astype(F32), lists)
    base = features + probes
    q1[base : base + LIST_ROWS] = jnp.concatenate([lists, jnp.zeros_like(lists)], 0).astype(BF16)
    q1[base + LIST_ROWS :] = leaf_skel[...].astype(F32).astype(BF16)


def own_kernel(points, leaf_skel, q2, lhs_t, rhs, lhs_c, rhs_c, near):
    leaves, features, size = points.shape
    for leaf in range(leaves):
        left = with_norms(points[leaf], True)
        right = with_norms(points[leaf], False)
        both = dot(
            jnp.concatenate([left, right], 0), one_hot(leaf_skel[leaf : leaf + 1, :], size), 1, 0
        )
        rhs[leaf] = right
        lhs_t[leaf] = left.T
        lhs_c[leaf] = both[: features + AUG].T.astype(BF16)
        rhs_c[leaf] = both[features + AUG :].astype(BF16)
    for leaf in range(leaves):
        block = tile(lhs_t[leaf], rhs[leaf], 1, 0)
        near[leaf] = dot(q2[leaf, :, :size], block, 1, 1)


def node_kernel(features, probes, cap, far_cap, mine, one, two, three, basis, skel, node, lists, q1):
    skeleton = mine.shape[1]
    leaves = mine.shape[0] - features - probes - LIST_ROWS
    shift = leaves.bit_length() - 1
    groups = 4
    me = lax.axis_index("sub")
    for rel, ref in enumerate((mine, one, two, three)):
        q1[rel] = ref[...]
    weights = jnp.zeros((probes, skeleton), F32)
    coords = jnp.zeros((features, skeleton), F32)
    for spot in range(groups):
        block = q1[jnp.bitwise_xor(me, spot)]
        span = slice(spot * skeleton, (spot + 1) * skeleton)
        weights += dot(block[features : features + probes], basis[0, :, span], 1, 1)
        coords += dot(block[:features], one_hot(skel[...], skeleton, spot * skeleton), 1, 0)
    node[:features] = coords.astype(BF16)
    node[features:] = weights.astype(BF16)

    base = features + probes
    lane = lax.broadcasted_iota(jnp.int32, (1, skeleton), 1)
    rows = [q1[rel, base : base + LIST_ROWS].astype(F32) for rel in range(groups)]
    whole = [block.astype(jnp.int32) for block in rows]
    segments = []
    for kind, limit in ((0, cap), (2, far_cap)):
        for rel in (None, 0, 1, 2, 3):
            block = whole[0 if rel is None else rel]
            first = block[kind : kind + 1]
            second = block[kind + 1 : kind + 2]
            used = lane < (block[4:5] if kind == 0 else limit)
            owner = second >> shift
            inner = second & (leaves - 1)
            if rel is None:
                apart = jnp.bitwise_xor(owner, me)
                own, slot = first, (apart & 1) * leaves + inner
                crosses = apart >= 2
                segments.append((kind, 0, own, slot, used & jnp.logical_not(crosses)))
                segments.append((kind, 1, own, slot, used & crosses))
            else:
                own, slot = inner, (rel & 1) * leaves + first
                segments.append((kind, rel >> 1, own, slot, used & (owner == me)))
    masks = jnp.concatenate([jnp.where(part[4], 1.0, 0.0) for part in segments], 0)
    count = len(segments)
    padded = -count % 16
    masks = jnp.concatenate([masks, jnp.zeros((padded, skeleton), F32)], 0)
    before = lax.broadcasted_iota(jnp.int32, (skeleton, skeleton), 0) < lax.broadcasted_iota(
        jnp.int32, (skeleton, skeleton), 1
    )
    prefix = dot(masks.astype(BF16), jnp.where(before, 1.0, 0.0).astype(BF16), 1, 0)
    totals = jnp.sum(masks, axis=1, keepdims=True)
    width = lists.shape[1]
    for kind in (0, 2):
        for cross in (0, 1):
            offset = jnp.zeros((1, 1), F32)
            result = jnp.zeros((8, width), F32)
            for index, part in enumerate(segments):
                if part[0] != kind or part[1] != cross:
                    continue
                place = jnp.where(part[4], prefix[index : index + 1] + offset, -1.0)
                offset += totals[index : index + 1]
                spots = lax.broadcasted_iota(jnp.int32, (width, skeleton), 0)
                hot = jnp.where(spots == place.astype(jnp.int32), 1.0, 0.0).astype(BF16)
                values = jnp.concatenate(
                    [part[2].astype(F32), part[3].astype(F32), jnp.zeros((6, skeleton), F32)], 0
                ).astype(BF16)
                result += dot(values, hot, 1, 1)
            line = kind + cross
            lists[2 * line : 2 * line + 2] = result[:2].astype(jnp.int32)
            lists[8 + line : 9 + line] = jnp.broadcast_to(offset, (1, width)).astype(jnp.int32)
    lists[12:] = jnp.zeros((4, width), jnp.int32)


def level_kernel(features, height, mine, other, basis, skel, node, pair):
    skeleton = mine.shape[1]
    on_right = (lax.axis_index("leaf") >> (height - 1)) & 1
    pair[0] = mine[...]
    pair[1] = other[...]
    left = pair[on_right]
    right = pair[1 - on_right]
    line = skel[0, height - 1 : height, :]
    weights = dot(left[features:], basis[0, height - 1, :, :skeleton], 1, 1)
    weights += dot(right[features:], basis[0, height - 1, :, skeleton:], 1, 1)
    coords = dot(left[:features], one_hot(line, skeleton), 1, 0)
    coords += dot(right[:features], one_hot(line, skeleton, skeleton), 1, 0)
    node[:features] = coords.astype(BF16)
    node[features:] = weights.astype(BF16)


def down_kernel(features, levels, *refs):
    nodes, refs = refs[: 2 * levels], refs[2 * levels :]
    upper_basis, subtree_basis, dev_basis, potentials = refs
    skeleton = nodes[0].shape[1]
    me = lax.axis_index("sub")
    subtree = lax.axis_index("leaf")
    far = []
    for level in range(levels):
        mine, other = nodes[2 * level], nodes[2 * level + 1]
        block = tile(
            with_norms(mine[:features], True), with_norms(other[:features], False), 0, 0
        )
        far.append(dot(other[features:], block, 1, 1))
    potential = far[levels - 1]
    for height in range(levels - 1, 0, -1):
        side = pl.multiple_of(((subtree >> (height - 1)) & 1) * skeleton, skeleton)
        part = upper_basis[0, height - 1, :, pl.ds(side, skeleton)]
        potential = far[height - 1] + dot(potential.astype(BF16), part, 1, 0)
    spot = pl.multiple_of(me * skeleton, skeleton)
    device = dot(potential.astype(BF16), subtree_basis[0, :, pl.ds(spot, skeleton)], 1, 0)
    spread = dot(device.astype(BF16), dev_basis[0], 1, 0).astype(BF16)
    for leaf in range(potentials.shape[0]):
        potentials[leaf] = spread[:, leaf * skeleton : (leaf + 1) * skeleton]


def build_sources(rhs, rhs_c, q1, base, features, probes, leaves):
    size = rhs.shape[2]
    skels = q1[features + probes + LIST_ROWS :].astype(F32).astype(jnp.int32)
    for leaf in range(leaves):
        right = with_norms(rhs[base + leaf, :features], False)
        rhs[base + leaf, features:] = right[features:]
        rhs_c[base + leaf] = dot(right, one_hot(skels[leaf : leaf + 1], size), 1, 0).astype(BF16)


def pair_sums(cross, lists, lhs_t, lhs_c, rhs, rhs_c, sw, near, far):
    size = rhs.shape[2]
    skeleton = rhs_c.shape[2]
    line = cross
    count = lists[8 + line, 0]

    def near_step(step, carry):
        results = []
        for index in range(NEAR_STEP):
            spot = step * NEAR_STEP + index
            own, slot = lists[2 * line, spot], lists[2 * line + 1, spot]
            block = tile(lhs_t[own], rhs[slot], 1, 0)
            part = dot(sw[slot, :, :size], block, 1, 1)
            results.append((own, jnp.where(spot < count, part, 0.0)))
        for own, part in results:
            near[own] += part
        return carry

    lax.fori_loop(0, (count + NEAR_STEP - 1) // NEAR_STEP, near_step, 0)
    far_line = 2 + cross
    far_count = lists[8 + far_line, 0]

    def far_step(step, carry):
        results = []
        for index in range(0, FAR_STEP, 2):
            spots = [step * FAR_STEP + index + half for half in range(2)]
            owns = [lists[2 * far_line, spot] for spot in spots]
            slots = [lists[2 * far_line + 1, spot] for spot in spots]
            blocks = [tile(lhs_c[own], rhs_c[slot], 1, 0) for own, slot in zip(owns, slots)]
            weights = jnp.concatenate([sw[slot, :, size:] for slot in slots], 0)
            part = dot(weights, jnp.concatenate(blocks, 0), 1, 1)
            probes = part.shape[0] // 2
            for half in range(2):
                mine = part[half * probes : (half + 1) * probes, half * skeleton : (half + 1) * skeleton]
                mine = mine.astype(BF16).astype(F32)
                results.append((owns[half], jnp.where(spots[half] < far_count, mine, 0.0)))
        for own, part in results:
            far[own] += part
        return carry

    lax.fori_loop(0, (far_count + FAR_STEP - 1) // FAR_STEP, far_step, 0)


def chip_kernel(
    features, lists, q1, lhs_t, lhs_c, own_rhs, own_rhs_c, own_q2, points, q2, near_in,
    near, far, rhs, rhs_c, sw, sems,
):
    leaves = own_rhs.shape[0]
    probes = q2.shape[1]
    copies = [
        pltpu.make_async_copy(points, rhs.at[pl.ds(leaves, leaves), pl.ds(0, features)], sems.at[0]),
        pltpu.make_async_copy(own_rhs, rhs.at[pl.ds(0, leaves)], sems.at[1]),
        pltpu.make_async_copy(own_rhs_c, rhs_c.at[pl.ds(0, leaves)], sems.at[2]),
        pltpu.make_async_copy(own_q2, sw.at[pl.ds(0, leaves)], sems.at[3]),
        pltpu.make_async_copy(q2, sw.at[pl.ds(leaves, leaves)], sems.at[4]),
    ]
    for copy in copies:
        copy.start()
    near[...] = near_in[...]
    far[...] = jnp.zeros_like(far)
    copies[0].wait()
    build_sources(rhs, rhs_c, q1, leaves, features, probes, leaves)
    for copy in copies[1:]:
        copy.wait()
    pair_sums(0, lists, lhs_t, lhs_c, rhs, rhs_c, sw, near, far)


def cross_kernel(
    features, lists, q1_two, q1_three, lhs_t, lhs_c, points_two, points_three, q2_two, q2_three,
    near_in, far_in, potentials, leaf_basis,
    out, near, far, rhs, rhs_c, sw, basis, sems,
):
    leaves = points_two.shape[0]
    probes = q2_two.shape[1]
    copies = []
    for index, (source, signs) in enumerate(((points_two, q2_two), (points_three, q2_three))):
        span = pl.ds(index * leaves, leaves)
        copies.append(
            pltpu.make_async_copy(source, rhs.at[span, pl.ds(0, features)], sems.at[2 * index])
        )
        copies.append(pltpu.make_async_copy(signs, sw.at[span], sems.at[2 * index + 1]))
    copies.append(pltpu.make_async_copy(leaf_basis, basis, sems.at[4]))
    for copy in copies:
        copy.start()
    near[...] = near_in[...]
    far[...] = far_in[...]
    copies[0].wait()
    build_sources(rhs, rhs_c, q1_two, 0, features, probes, leaves)
    copies[2].wait()
    build_sources(rhs, rhs_c, q1_three, leaves, features, probes, leaves)
    copies[1].wait()
    copies[3].wait()
    pair_sums(1, lists, lhs_t, lhs_c, rhs, rhs_c, sw, near, far)
    copies[4].wait()
    for leaf in range(leaves):
        total = potentials[leaf].astype(F32) + far[leaf]
        high = total.astype(BF16)
        low = (total - high.astype(F32)).astype(BF16)
        part = dot(jnp.concatenate([high, low], 0), basis[leaf], 1, 0)
        out[leaf] = near[leaf] + part[:probes] + part[probes:]


def call(kernel, name, out_shape, in_specs, scratch, micros, *args):
    return pl.pallas_call(
        kernel,
        name=name,
        out_shape=out_shape,
        in_specs=in_specs,
        out_specs=jax.tree.map(lambda _: VMEM, out_shape),
        scratch_shapes=scratch,
        compiler_params=pltpu.CompilerParams(vmem_limit_bytes=VMEM_LIMIT),
        cost_estimate=pl.CostEstimate(
            flops=int(micros * 1e9), bytes_accessed=int(micros * 1e6), transcendentals=0
        ),
    )(*args)


def on_device(
    points,
    probe_bits,
    leaf_skel,
    leaf_basis,
    device_skel,
    device_basis,
    subtree_skel,
    subtree_basis,
    upper_skel,
    upper_basis,
    near_pairs,
    near_count,
    far_pairs,
):
    leaves, features, size = points.shape
    probes = probe_bits.shape[1]
    skeleton = leaf_skel.shape[1]
    levels = lax.axis_size("leaf").bit_length() - 1
    cap = near_pairs.shape[1]
    far_cap = far_pairs.shape[1]
    depth = features + AUG
    width = max(-(-3 * cap // 128), -(-3 * far_cap // 128)) * 128
    q1_rows = features + probes + LIST_ROWS + leaves
    shape = jax.ShapeDtypeStruct

    points_two = flipped(points, "sub", 2)
    points_one = flipped(points, "sub", 1)

    q1, q2 = call(
        prep_kernel,
        "prep",
        (shape((q1_rows, skeleton), BF16), shape((leaves, probes, size + skeleton), BF16)),
        [VMEM] * 7 + [SMEM, VMEM],
        [],
        4,
        points,
        probe_bits,
        leaf_skel,
        leaf_basis,
        device_skel,
        device_basis,
        near_pairs,
        near_count,
        far_pairs,
    )
    q1_one, q1_two, q1_three = (flipped(q1, "sub", bits) for bits in (1, 2, 3))
    q2_two = flipped(q2, "sub", 2)
    q2_one = flipped(q2, "sub", 1)

    lhs_t, rhs, lhs_c, rhs_c, near = call(
        own_kernel,
        "own",
        (
            shape((leaves, size, depth), BF16),
            shape((leaves, depth, size), BF16),
            shape((leaves, skeleton, depth), BF16),
            shape((leaves, depth, skeleton), BF16),
            shape((leaves, probes, size), F32),
        ),
        [VMEM] * 3,
        [],
        5,
        points,
        leaf_skel,
        q2,
    )

    node, lists = call(
        functools.partial(node_kernel, features, probes, cap, far_cap),
        "node",
        (shape((features + probes, skeleton), BF16), shape((16, width), jnp.int32)),
        [VMEM] * 6,
        [pltpu.VMEM((4, q1_rows, skeleton), BF16)],
        2,
        q1,
        q1_one,
        q1_two,
        q1_three,
        subtree_basis,
        subtree_skel,
    )
    nodes = []
    for height in range(1, levels + 1):
        other = flipped(node, "leaf", 1 << (height - 1))
        nodes += [node, other]
        if height < levels:
            node = call(
                functools.partial(level_kernel, features, height),
                f"level{height}",
                shape((features + probes, skeleton), BF16),
                [VMEM] * 4,
                [pltpu.VMEM((2, features + probes, skeleton), BF16)],
                1,
                node,
                other,
                upper_basis,
                upper_skel,
            )

    near, far = call(
        functools.partial(chip_kernel, features),
        "chip",
        (shape((leaves, probes, size), F32), shape((leaves, probes, skeleton), F32)),
        [SMEM, VMEM, VMEM, VMEM] + [ANY] * 5 + [VMEM],
        [
            pltpu.VMEM((2 * leaves, depth, size), BF16),
            pltpu.VMEM((2 * leaves, depth, skeleton), BF16),
            pltpu.VMEM((2 * leaves, probes, size + skeleton), BF16),
            pltpu.SemaphoreType.DMA((5,)),
        ],
        10,
        lists,
        q1_one,
        lhs_t,
        lhs_c,
        rhs,
        rhs_c,
        q2,
        points_one,
        q2_one,
        near,
    )

    potentials = call(
        functools.partial(down_kernel, features, levels),
        "down",
        shape((leaves, probes, skeleton), BF16),
        [VMEM] * (2 * levels + 3),
        [],
        2,
        *nodes,
        upper_basis,
        subtree_basis,
        device_basis,
    )

    points_three = flipped(points_two, "sub", 1)
    q2_three = flipped(q2_two, "sub", 1)
    return call(
        functools.partial(cross_kernel, features),
        "cross",
        shape((leaves, probes, size), F32),
        [SMEM] + [VMEM] * 4 + [ANY] * 4 + [VMEM] * 3 + [ANY],
        [
            pltpu.VMEM((leaves, probes, size), F32),
            pltpu.VMEM((leaves, probes, skeleton), F32),
            pltpu.VMEM((2 * leaves, depth, size), BF16),
            pltpu.VMEM((2 * leaves, depth, skeleton), BF16),
            pltpu.VMEM((2 * leaves, probes, size + skeleton), BF16),
            pltpu.VMEM((leaves, skeleton, size), BF16),
            pltpu.SemaphoreType.DMA((5,)),
        ],
        10,
        lists,
        q1_two,
        q1_three,
        lhs_t,
        lhs_c,
        points_two,
        points_three,
        q2_two,
        q2_three,
        near,
        far,
        potentials,
        leaf_basis,
    )


def solution(mesh):
    return jax.shard_map(
        on_device,
        mesh=mesh,
        in_specs=(
            P(("leaf", "sub"), None, None),
            P(("leaf", "sub"), None, None),
            P(("leaf", "sub"), None),
            P(("leaf", "sub"), None, None),
            P(("leaf", "sub"), None),
            P(("leaf", "sub"), None, None),
            P("leaf", None),
            P("leaf", None, None),
            P("leaf", None, None),
            P("leaf", None, None, None),
            P(("leaf", "sub"), None, None),
            P(("leaf", "sub")),
            P(("leaf", "sub"), None, None),
        ),
        out_specs=P(("leaf", "sub"), None, None),
        check_vma=False,
    )
```

```python
import functools

import jax
import jax.numpy as jnp
from jax import lax
from jax.experimental import pallas as pl
from jax.experimental.pallas import tpu as pltpu
from jax.sharding import PartitionSpec as P


BF16 = jnp.bfloat16
F32 = jnp.float32
AUG = 16
NEAR_STEP = 16
FAR_STEP = 32
LIST_ROWS = 16
VMEM = pl.BlockSpec(memory_space=pltpu.VMEM)
SMEM = pl.BlockSpec(memory_space=pltpu.SMEM)
ANY = pl.BlockSpec(memory_space=pl.ANY)
VMEM_LIMIT = 24 << 20
TOKEN = (8, 128)


def flipped(block, axis, bits):
    count = lax.axis_size(axis)
    return lax.ppermute(block, axis, [(low, low ^ bits) for low in range(count)])


def dot(left, right, left_dim, right_dim):
    return lax.dot_general(
        left, right, (((left_dim,), (right_dim,)), ((), ())), preferred_element_type=F32
    )


def one_hot(columns, rows, start=0):
    spots = lax.broadcasted_iota(jnp.int32, (rows, columns.shape[1]), 0) + start
    return jnp.where(spots == columns, 1.0, 0.0).astype(BF16)


def norm_parts(coords):
    wide = coords.astype(F32)
    norm = jnp.sum(wide * wide, axis=0, keepdims=True) * (-1.0 / coords.shape[0])
    high = norm.astype(BF16).astype(F32)
    rest = norm - high
    middle = rest.astype(BF16).astype(F32)
    return high, middle, rest - middle


def aug_rows(parts, width, norm_first):
    row = lax.broadcasted_iota(jnp.int32, (AUG, width), 0)
    start, ones = (0, 3) if norm_first else (3, 0)
    block = jnp.where((row >= ones) & (row < ones + 3), 1.0, 0.0)
    for index, part in enumerate(parts):
        block = jnp.where(row == start + index, part, block)
    return block.astype(BF16)


def with_norms(coords, norm_first):
    rows = aug_rows(norm_parts(coords), coords.shape[1], norm_first)
    scaled = (coords.astype(F32) * (2.0 / coords.shape[0])).astype(BF16) if norm_first else coords
    return jnp.concatenate([scaled, rows], axis=0)


def tile(left, right, left_dim, right_dim):
    return jnp.exp(dot(left, right, left_dim, right_dim)).astype(BF16)


def list_rows(pairs, row, width):
    pick = lax.broadcasted_iota(jnp.int32, (8, 2), 0) == lax.broadcasted_iota(
        jnp.int32, (8, 2), 1
    ) + row
    spread = jnp.where(pick, 1.0, 0.0).astype(BF16)
    rows = dot(spread, pairs.astype(F32).astype(BF16), 1, 0)
    short = width - pairs.shape[1]
    return jnp.concatenate([rows, jnp.zeros((8, short), F32)], axis=1) if short else rows


def prep_kernel(
    points, bits, leaf_skel, leaf_basis, dev_skel, dev_basis, near, near_count, far, q1, q2
):
    leaves, features, size = points.shape
    probes = bits.shape[1]
    skeleton = leaf_skel.shape[1]
    node_weights = jnp.zeros((probes, skeleton), F32)
    node_coords = jnp.zeros((features, skeleton), F32)
    for leaf in range(leaves):
        span = slice(leaf * skeleton, (leaf + 1) * skeleton)
        signs = (2 * bits[leaf] - 1).astype(F32).astype(BF16)
        q2[leaf, :, :size] = signs
        weights = dot(signs, leaf_basis[leaf], 1, 1).astype(BF16)
        q2[leaf, :, size:] = weights
        node_weights += dot(weights, dev_basis[0, :, span], 1, 1)
        coords = dot(points[leaf], one_hot(leaf_skel[leaf : leaf + 1, :], size), 1, 0).astype(BF16)
        node_coords += dot(coords, one_hot(dev_skel[...], skeleton, leaf * skeleton), 1, 0)
    q1[:features] = node_coords.astype(BF16)
    q1[features : features + probes] = node_weights.astype(BF16)
    lists = list_rows(near[0], 0, skeleton) + list_rows(far[0], 2, skeleton)
    row = lax.broadcasted_iota(jnp.int32, lists.shape, 0)
    lists = jnp.where(row == 4, near_count[0].astype(F32), lists)
    base = features + probes
    q1[base : base + LIST_ROWS] = jnp.concatenate([lists, jnp.zeros_like(lists)], 0).astype(BF16)
    q1[base + LIST_ROWS :] = leaf_skel[...].astype(F32).astype(BF16)


def own_kernel(points, leaf_skel, q2, lhs_t, lhs_c, rhs, rhs_c, sw, near, token):
    leaves, features, size = points.shape
    for leaf in range(leaves):
        left = with_norms(points[leaf], True)
        right = with_norms(points[leaf], False)
        both = dot(
            jnp.concatenate([left, right], 0), one_hot(leaf_skel[leaf : leaf + 1, :], size), 1, 0
        )
        rhs[leaf] = right
        lhs_t[leaf] = left.T
        lhs_c[leaf] = both[: features + AUG].T.astype(BF16)
        rhs_c[leaf] = both[features + AUG :].astype(BF16)
        sw[leaf] = q2[leaf]
    for leaf in range(leaves):
        block = tile(lhs_t[leaf], rhs[leaf], 1, 0)
        near[leaf] = dot(q2[leaf, :, :size], block, 1, 1)
    token[...] = jnp.zeros_like(token)


def node_kernel(
    features, probes, cap, far_cap, mine, one, two, three, basis, skel, token, node, lists, q1
):
    skeleton = mine.shape[1]
    leaves = mine.shape[0] - features - probes - LIST_ROWS
    shift = leaves.bit_length() - 1
    groups = 4
    me = lax.axis_index("sub")
    for rel, ref in enumerate((mine, one, two, three)):
        q1[rel] = ref[...]
    weights = jnp.zeros((probes, skeleton), F32)
    coords = jnp.zeros((features, skeleton), F32)
    for spot in range(groups):
        block = q1[jnp.bitwise_xor(me, spot)]
        span = slice(spot * skeleton, (spot + 1) * skeleton)
        weights += dot(block[features : features + probes], basis[0, :, span], 1, 1)
        coords += dot(block[:features], one_hot(skel[...], skeleton, spot * skeleton), 1, 0)
    node[:features] = coords.astype(BF16)
    node[features:] = weights.astype(BF16)

    base = features + probes
    lane = lax.broadcasted_iota(jnp.int32, (1, skeleton), 1)
    rows = [q1[rel, base : base + LIST_ROWS].astype(F32) for rel in range(groups)]
    whole = [block.astype(jnp.int32) for block in rows]
    segments = []
    for kind, limit in ((0, cap), (2, far_cap)):
        for rel in (None, 0, 1, 2, 3):
            block = whole[0 if rel is None else rel]
            first = block[kind : kind + 1]
            second = block[kind + 1 : kind + 2]
            used = lane < (block[4:5] if kind == 0 else limit)
            owner = second >> shift
            inner = second & (leaves - 1)
            if rel is not None:
                line = 0 if kind == 0 else 1 + (rel >> 1)
                segments.append((line, inner, rel * leaves + first, used & (owner == me)))
                continue
            apart = jnp.bitwise_xor(owner, me)
            slot = apart * leaves + inner
            if kind == 0:
                segments.append((0, first, slot, used))
            else:
                segments.append((1, first, slot, used & (apart < 2)))
                segments.append((2, first, slot, used & (apart >= 2)))
    masks = jnp.concatenate([jnp.where(part[3], 1.0, 0.0) for part in segments], 0)
    masks = jnp.concatenate([masks, jnp.zeros((-len(segments) % 16, skeleton), F32)], 0)
    before = lax.broadcasted_iota(jnp.int32, (skeleton, skeleton), 0) < lax.broadcasted_iota(
        jnp.int32, (skeleton, skeleton), 1
    )
    prefix = dot(masks.astype(BF16), jnp.where(before, 1.0, 0.0).astype(BF16), 1, 0)
    totals = jnp.sum(masks, axis=1, keepdims=True)
    width = lists.shape[1]
    for line in range(3):
        offset = jnp.zeros((1, 1), F32)
        result = jnp.zeros((8, width), F32)
        for index, part in enumerate(segments):
            if part[0] != line:
                continue
            place = jnp.where(part[3], prefix[index : index + 1] + offset, -1.0)
            offset += totals[index : index + 1]
            spots = lax.broadcasted_iota(jnp.int32, (width, skeleton), 0)
            hot = jnp.where(spots == place.astype(jnp.int32), 1.0, 0.0).astype(BF16)
            values = jnp.concatenate(
                [part[1].astype(F32), part[2].astype(F32), jnp.zeros((6, skeleton), F32)], 0
            ).astype(BF16)
            result += dot(values, hot, 1, 1)
        lists[2 * line : 2 * line + 2] = result[:2].astype(jnp.int32)
        lists[8 + line : 9 + line] = jnp.broadcast_to(offset, (1, width)).astype(jnp.int32)
    lists[6:8] = jnp.zeros((2, width), jnp.int32)
    lists[11:] = jnp.zeros((5, width), jnp.int32)


def build(rel, points, q1, q2, rhs, rhs_c, sw):
    leaves, _, size = points.shape
    base = rel * leaves
    skels = q1[q1.shape[0] - leaves :].astype(F32).astype(jnp.int32)
    for leaf in range(leaves):
        right = with_norms(points[leaf], False)
        rhs[base + leaf] = right
        rhs_c[base + leaf] = dot(right, one_hot(skels[leaf : leaf + 1], size), 1, 0).astype(BF16)
        sw[base + leaf] = q2[leaf]


def level_kernel(features, height, mine, other, basis, skel, after, node, pair):
    skeleton = mine.shape[1]
    on_right = (lax.axis_index("leaf") >> (height - 1)) & 1
    pair[0] = mine[...]
    pair[1] = other[...]
    left = pair[on_right]
    right = pair[1 - on_right]
    line = skel[0, height - 1 : height, :]
    weights = dot(left[features:], basis[0, height - 1, :, :skeleton], 1, 1)
    weights += dot(right[features:], basis[0, height - 1, :, skeleton:], 1, 1)
    coords = dot(left[:features], one_hot(line, skeleton), 1, 0)
    coords += dot(right[:features], one_hot(line, skeleton, skeleton), 1, 0)
    node[:features] = coords.astype(BF16)
    node[features:] = weights.astype(BF16)


def far_sums(line, size, lists, lhs_c, rhs_c, sw, far):
    skeleton = rhs_c.shape[2]
    count = lists[8 + line, 0]

    def step_of(step, carry):
        results = []
        for index in range(0, FAR_STEP, 2):
            spots = [step * FAR_STEP + index + half for half in range(2)]
            owns = [lists[2 * line, spot] for spot in spots]
            slots = [lists[2 * line + 1, spot] for spot in spots]
            blocks = [tile(lhs_c[own], rhs_c[slot], 1, 0) for own, slot in zip(owns, slots)]
            weights = jnp.concatenate([sw[slot, :, size:] for slot in slots], 0)
            part = dot(weights, jnp.concatenate(blocks, 0), 1, 1)
            probes = part.shape[0] // 2
            for half in range(2):
                rows = slice(half * probes, (half + 1) * probes)
                mine = part[rows, half * skeleton : (half + 1) * skeleton]
                mine = mine.astype(BF16).astype(F32)
                results.append((owns[half], jnp.where(spots[half] < count, mine, 0.0)))
        for own, part in results:
            far[own] += part
        return carry

    lax.fori_loop(0, (count + FAR_STEP - 1) // FAR_STEP, step_of, 0)


def near_sums(size, lists, lhs_t, rhs, sw, near):
    count = lists[8, 0]

    def step_of(step, carry):
        results = []
        for index in range(NEAR_STEP):
            spot = step * NEAR_STEP + index
            own, slot = lists[0, spot], lists[1, spot]
            block = tile(lhs_t[own], rhs[slot], 1, 0)
            part = dot(sw[slot, :, :size], block, 1, 1)
            results.append((own, jnp.where(spot < count, part, 0.0)))
        for own, part in results:
            near[own] += part
        return carry

    lax.fori_loop(0, (count + NEAR_STEP - 1) // NEAR_STEP, step_of, 0)


def first_kernel(points, q1, q2, lists, lhs_c, _, __, ___, rhs, rhs_c, sw, far):
    build(1, points, q1, q2, rhs, rhs_c, sw)
    far[...] = jnp.zeros_like(far)
    far_sums(1, points.shape[2], lists, lhs_c, rhs_c, sw, far)


def second_kernel(points, q1, q2, after, _, __, ___, rhs, rhs_c, sw, token):
    build(2, points, q1, q2, rhs, rhs_c, sw)
    token[...] = jnp.zeros_like(token)


def third_kernel(points, q1, q2, lists, lhs_c, after, _, __, ___, ____, rhs, rhs_c, sw, far):
    build(3, points, q1, q2, rhs, rhs_c, sw)
    far_sums(2, points.shape[2], lists, lhs_c, rhs_c, sw, far)


def last_kernel(features, levels, *refs):
    nodes, refs = refs[: 2 * levels], refs[2 * levels :]
    upper_basis, subtree_basis, dev_basis, leaf_basis, lists, lhs_t, rhs, sw, far, near, out = refs
    leaves, probes, size = out.shape
    skeleton = nodes[0].shape[1]
    me = lax.axis_index("sub")
    subtree = lax.axis_index("leaf")
    tree = []
    for level in range(levels):
        mine, other = nodes[2 * level], nodes[2 * level + 1]
        block = tile(
            with_norms(mine[:features], True), with_norms(other[:features], False), 0, 0
        )
        tree.append(dot(other[features:], block, 1, 1))
    potential = tree[levels - 1]
    for height in range(levels - 1, 0, -1):
        side = pl.multiple_of(((subtree >> (height - 1)) & 1) * skeleton, skeleton)
        part = upper_basis[0, height - 1, :, pl.ds(side, skeleton)]
        potential = tree[height - 1] + dot(potential.astype(BF16), part, 1, 0)
    spot = pl.multiple_of(me * skeleton, skeleton)
    device = dot(potential.astype(BF16), subtree_basis[0, :, pl.ds(spot, skeleton)], 1, 0)
    spread = dot(device.astype(BF16), dev_basis[0], 1, 0).astype(BF16)
    for leaf in range(leaves):
        total = spread[:, leaf * skeleton : (leaf + 1) * skeleton].astype(F32) + far[leaf]
        high = total.astype(BF16)
        low = (total - high.astype(F32)).astype(BF16)
        part = dot(jnp.concatenate([high, low], 0), leaf_basis[leaf], 1, 0)
        out[leaf] = near[leaf] + part[:probes] + part[probes:]
    near_sums(size, lists, lhs_t, rhs, sw, out)


def call(kernel, out_shape, in_specs, micros, *args, scratch=(), aliases=()):
    return pl.pallas_call(
        kernel,
        out_shape=out_shape,
        in_specs=in_specs,
        out_specs=jax.tree.map(lambda _: VMEM, out_shape),
        scratch_shapes=scratch,
        input_output_aliases=dict(aliases),
        compiler_params=pltpu.CompilerParams(vmem_limit_bytes=VMEM_LIMIT),
        cost_estimate=pl.CostEstimate(
            flops=int(micros * 1e9), bytes_accessed=int(micros * 1e6), transcendentals=0
        ),
    )(*args)


def on_device(
    points,
    probe_bits,
    leaf_skel,
    leaf_basis,
    device_skel,
    device_basis,
    subtree_skel,
    subtree_basis,
    upper_skel,
    upper_basis,
    near_pairs,
    near_count,
    far_pairs,
):
    leaves, features, size = points.shape
    probes = probe_bits.shape[1]
    skeleton = leaf_skel.shape[1]
    levels = lax.axis_size("leaf").bit_length() - 1
    cap = near_pairs.shape[1]
    far_cap = far_pairs.shape[1]
    depth = features + AUG
    width = max(-(-5 * cap // 128), -(-3 * far_cap // 128)) * 128
    q1_rows = features + probes + LIST_ROWS + leaves
    slots = 4 * leaves
    shape = jax.ShapeDtypeStruct
    rhs_shape = shape((slots, depth, size), BF16)
    rhs_c_shape = shape((slots, depth, skeleton), BF16)
    sw_shape = shape((slots, probes, size + skeleton), BF16)
    near_shape = shape((leaves, probes, size), F32)
    far_shape = shape((leaves, probes, skeleton), F32)
    node_shape = shape((features + probes, skeleton), BF16)
    token_shape = shape(TOKEN, F32)

    q1, q2 = call(
        prep_kernel,
        (shape((q1_rows, skeleton), BF16), shape((leaves, probes, size + skeleton), BF16)),
        [VMEM] * 7 + [SMEM, VMEM],
        4,
        points,
        probe_bits,
        leaf_skel,
        leaf_basis,
        device_skel,
        device_basis,
        jnp.swapaxes(near_pairs, 1, 2),
        near_count,
        jnp.swapaxes(far_pairs, 1, 2),
    )
    q1_one, q1_two, q1_three = (
        flipped(q1, "sub", bits) for bits in (1, 2, 3)
    )
    q2_two = flipped(q2, "sub", 2)
    points_two = flipped(points, "sub", 2)
    q2_one = flipped(q2, "sub", 1)
    points_one = flipped(points, "sub", 1)

    lhs_t, lhs_c, rhs, rhs_c, sw, near, token = call(
        own_kernel,
        (
            shape((leaves, size, depth), BF16),
            shape((leaves, skeleton, depth), BF16),
            rhs_shape,
            rhs_c_shape,
            sw_shape,
            near_shape,
            token_shape,
        ),
        [VMEM] * 3,
        5,
        points,
        leaf_skel,
        q2,
    )
    node, lists = call(
        functools.partial(node_kernel, features, probes, cap, far_cap),
        (node_shape, shape((16, width), jnp.int32)),
        [VMEM] * 6 + [ANY],
        2,
        q1,
        q1_one,
        q1_two,
        q1_three,
        subtree_basis,
        subtree_skel,
        token,
        scratch=[pltpu.VMEM((4, q1_rows, skeleton), BF16)],
    )
    nodes = []
    far = after = None
    for height in range(1, levels + 1):
        other = flipped(node, "leaf", 1 << (height - 1))
        nodes += [node, other]
        if height == 1:
            rhs, rhs_c, sw, far = call(
                first_kernel,
                (rhs_shape, rhs_c_shape, sw_shape, far_shape),
                [VMEM] * 3 + [SMEM, VMEM] + [ANY] * 3,
                5,
                points_one,
                q1_one,
                q2_one,
                lists,
                lhs_c,
                rhs,
                rhs_c,
                sw,
                aliases=((5, 0), (6, 1), (7, 2)),
            )
            after = far
        if height == 2:
            points_three = flipped(points_two, "sub", 1)
            q2_three = flipped(q2_two, "sub", 1)
            rhs, rhs_c, sw, after = call(
                second_kernel,
                (rhs_shape, rhs_c_shape, sw_shape, token_shape),
                [VMEM] * 3 + [ANY] * 4,
                2,
                points_two,
                q1_two,
                q2_two,
                node,
                rhs,
                rhs_c,
                sw,
                aliases=((4, 0), (5, 1), (6, 2)),
            )
        if height == 3:
            rhs, rhs_c, sw, far = call(
                third_kernel,
                (rhs_shape, rhs_c_shape, sw_shape, far_shape),
                [VMEM] * 3 + [SMEM, VMEM] + [ANY] * 4 + [VMEM],
                5,
                points_three,
                q1_three,
                q2_three,
                lists,
                lhs_c,
                node,
                rhs,
                rhs_c,
                sw,
                far,
                aliases=((6, 0), (7, 1), (8, 2), (9, 3)),
            )
            after = far
        if height < levels:
            node = call(
                functools.partial(level_kernel, features, height),
                node_shape,
                [VMEM] * 4 + [ANY],
                1,
                node,
                other,
                upper_basis,
                upper_skel,
                after,
                scratch=[pltpu.VMEM((2, features + probes, skeleton), BF16)],
            )

    return call(
        functools.partial(last_kernel, features, levels),
        near_shape,
        [VMEM] * (2 * levels + 4) + [SMEM] + [VMEM] * 5,
        10,
        *nodes,
        upper_basis,
        subtree_basis,
        device_basis,
        leaf_basis,
        lists,
        lhs_t,
        rhs,
        sw,
        far,
        near,
    )


def solution(mesh):
    return jax.shard_map(
        on_device,
        mesh=mesh,
        in_specs=(
            P(("leaf", "sub"), None, None),
            P(("leaf", "sub"), None, None),
            P(("leaf", "sub"), None),
            P(("leaf", "sub"), None, None),
            P(("leaf", "sub"), None),
            P(("leaf", "sub"), None, None),
            P("leaf", None),
            P("leaf", None, None),
            P("leaf", None, None),
            P("leaf", None, None, None),
            P(("leaf", "sub"), None, None),
            P(("leaf", "sub")),
            P(("leaf", "sub"), None, None),
        ),
        out_specs=P(("leaf", "sub"), None, None),
        check_vma=False,
    )
```

```python
import functools

import jax
import jax.numpy as jnp
from jax import lax
from jax.experimental import pallas as pl
from jax.experimental.pallas import tpu as pltpu
from jax.sharding import PartitionSpec as P


BF16 = jnp.bfloat16
F32 = jnp.float32
AUG = 16
NEAR_STEP = 16
OWN_STEP = 8
CHUNKS = 4
FAR_STEP = 32
LIST_ROWS = 16
VMEM = pl.BlockSpec(memory_space=pltpu.VMEM)
SMEM = pl.BlockSpec(memory_space=pltpu.SMEM)
ANY = pl.BlockSpec(memory_space=pl.ANY)
HBM = pl.BlockSpec(memory_space=pltpu.HBM)
VMEM_LIMIT = 24 << 20
TOKEN = (8, 128)


def flipped(block, axis, bits):
    count = lax.axis_size(axis)
    return lax.ppermute(block, axis, [(low, low ^ bits) for low in range(count)])


def dot(left, right, left_dim, right_dim):
    return lax.dot_general(
        left, right, (((left_dim,), (right_dim,)), ((), ())), preferred_element_type=F32
    )


def one_hot(columns, rows, start=0):
    spots = lax.broadcasted_iota(jnp.int32, (rows, columns.shape[1]), 0) + start
    return jnp.where(spots == columns, 1.0, 0.0).astype(BF16)


def norm_parts(coords):
    wide = coords.astype(F32)
    norm = jnp.sum(wide * wide, axis=0, keepdims=True) * (-1.0 / coords.shape[0])
    high = norm.astype(BF16).astype(F32)
    rest = norm - high
    middle = rest.astype(BF16).astype(F32)
    return high, middle, rest - middle


def aug_rows(parts, width, norm_first):
    row = lax.broadcasted_iota(jnp.int32, (AUG, width), 0)
    start, ones = (0, 3) if norm_first else (3, 0)
    block = jnp.where((row >= ones) & (row < ones + 3), 1.0, 0.0)
    for index, part in enumerate(parts):
        block = jnp.where(row == start + index, part, block)
    return block.astype(BF16)


def with_norms(coords, norm_first):
    rows = aug_rows(norm_parts(coords), coords.shape[1], norm_first)
    scaled = (coords.astype(F32) * (2.0 / coords.shape[0])).astype(BF16) if norm_first else coords
    return jnp.concatenate([scaled, rows], axis=0)


def tile(left, right, left_dim, right_dim):
    return jnp.exp(dot(left, right, left_dim, right_dim)).astype(BF16)


def list_rows(pairs, row, width):
    pick = lax.broadcasted_iota(jnp.int32, (8, 2), 0) == lax.broadcasted_iota(
        jnp.int32, (8, 2), 1
    ) + row
    spread = jnp.where(pick, 1.0, 0.0).astype(BF16)
    rows = dot(spread, pairs.astype(F32).astype(BF16), 1, 0)
    short = width - pairs.shape[1]
    return jnp.concatenate([rows, jnp.zeros((8, short), F32)], axis=1) if short else rows


def prep_kernel(
    points_in, bits_in, skel_in, basis_in, dev_skel_in, dev_basis_in, near_in, near_count, far_in,
    q1, q2, points, bits, leaf_skel, leaf_basis, dev_skel, dev_basis, near, far, sems,
):
    leaves, features, size = points.shape
    probes = bits.shape[1]
    skeleton = leaf_skel.shape[1]
    small = [
        pltpu.make_async_copy(source, target, sems.at[index])
        for index, (source, target) in enumerate(
            ((skel_in, leaf_skel), (dev_skel_in, dev_skel), (near_in, near), (far_in, far))
        )
    ]
    chunk = leaves // CHUNKS
    large = []
    for index in range(CHUNKS):
        rows = pl.ds(index * chunk, chunk)
        columns = pl.ds(index * chunk * skeleton, chunk * skeleton)
        base = 4 + 4 * index
        large.append(
            [
                pltpu.make_async_copy(points_in.at[rows], points.at[rows], sems.at[base]),
                pltpu.make_async_copy(bits_in.at[rows], bits.at[rows], sems.at[base + 1]),
                pltpu.make_async_copy(basis_in.at[rows], leaf_basis.at[rows], sems.at[base + 2]),
                pltpu.make_async_copy(
                    dev_basis_in.at[0, :, columns], dev_basis.at[:, columns], sems.at[base + 3]
                ),
            ]
        )
    for copy in small + [copy for group in large for copy in group]:
        copy.start()
    for copy in small:
        copy.wait()
    names = jnp.concatenate(
        [leaf_skel[...].astype(F32), jnp.broadcast_to(dev_skel[...].astype(F32), (8, skeleton))], 0
    ).T
    lane = lax.broadcasted_iota(jnp.int32, (skeleton, size), 1).astype(F32)
    total = jnp.zeros((features + probes, size), F32)
    for first in range(0, leaves, 2):
        if first % chunk == 0:
            for copy in large[first // chunk]:
                copy.wait()
        coords, weights = [], []
        for leaf in (first, first + 1):
            signs = (2 * bits[leaf] - 1).astype(F32).astype(BF16)
            hot = jnp.where(lane == names[:, leaf : leaf + 1], 1.0, 0.0).astype(BF16)
            both = dot(
                jnp.concatenate([points[leaf], signs], 0),
                jnp.concatenate([hot, leaf_basis[leaf]], 0),
                1,
                1,
            ).astype(BF16)
            coords.append(both[:features, :skeleton])
            weights.append(both[features:, skeleton:])
            q2[leaf, :, :size] = signs
            q2[leaf, :, size:] = weights[-1]
        spots = lane + float(first * skeleton)
        hot = jnp.where(spots == names[:, leaves : leaves + 1], 1.0, 0.0).astype(BF16)
        columns = slice(first * skeleton, (first + 2) * skeleton)
        total += dot(
            jnp.concatenate([jnp.concatenate(coords, 1), jnp.concatenate(weights, 1)], 0),
            jnp.concatenate([hot, dev_basis[:, columns]], 0),
            1,
            1,
        )
    q1[:features] = total[:features, :skeleton].astype(BF16)
    q1[features : features + probes] = total[features:, skeleton:].astype(BF16)
    lists = list_rows(near[0], 0, skeleton) + list_rows(far[0], 2, skeleton)
    row = lax.broadcasted_iota(jnp.int32, lists.shape, 0)
    lists = jnp.where(row == 4, near_count[0].astype(F32), lists)
    base = features + probes
    q1[base : base + LIST_ROWS] = jnp.concatenate([lists, jnp.zeros_like(lists)], 0).astype(BF16)
    q1[base + LIST_ROWS :] = leaf_skel[...].astype(F32).astype(BF16)


def own_kernel(points, leaf_skel, q2, lhs_t, lhs_c, rhs, rhs_c, sw, near, token):
    leaves, features, size = points.shape
    for leaf in range(leaves):
        left = with_norms(points[leaf], True)
        right = with_norms(points[leaf], False)
        both = dot(
            jnp.concatenate([left, right], 0), one_hot(leaf_skel[leaf : leaf + 1, :], size), 1, 0
        ).astype(BF16)
        rhs[leaf] = right
        lhs_t[leaf] = left.T
        lhs_c[leaf] = both[: features + AUG].T
        rhs_c[leaf] = both[features + AUG :]
        sw[leaf] = q2[leaf]

    def step_of(step, carry):
        for index in range(OWN_STEP):
            leaf = step * OWN_STEP + index
            block = tile(lhs_t[leaf], rhs[leaf], 1, 0)
            near[leaf] = dot(q2[leaf, :, :size], block, 1, 1)
        return carry

    lax.fori_loop(0, leaves // OWN_STEP, step_of, 0)
    token[...] = jnp.zeros_like(token)


def node_kernel(
    features, probes, cap, far_cap, mine, one, two, three, basis, skel, token, node, lists, q1
):
    skeleton = mine.shape[1]
    leaves = mine.shape[0] - features - probes - LIST_ROWS
    shift = leaves.bit_length() - 1
    groups = 4
    me = lax.axis_index("sub")
    for rel, ref in enumerate((mine, one, two, three)):
        q1[rel] = ref[...]
    weights = jnp.zeros((probes, skeleton), F32)
    coords = jnp.zeros((features, skeleton), F32)
    for spot in range(groups):
        block = q1[jnp.bitwise_xor(me, spot)]
        span = slice(spot * skeleton, (spot + 1) * skeleton)
        weights += dot(block[features : features + probes], basis[0, :, span], 1, 1)
        coords += dot(block[:features], one_hot(skel[...], skeleton, spot * skeleton), 1, 0)
    node[:features] = coords.astype(BF16)
    node[features:] = weights.astype(BF16)

    base = features + probes
    lane = lax.broadcasted_iota(jnp.int32, (1, skeleton), 1)
    rows = [q1[rel, base : base + LIST_ROWS].astype(F32) for rel in range(groups)]
    whole = [block.astype(jnp.int32) for block in rows]
    segments = []
    for kind, limit in ((0, cap), (2, far_cap)):
        for rel in (None, 0, 1, 2, 3):
            block = whole[0 if rel is None else rel]
            first = block[kind : kind + 1]
            second = block[kind + 1 : kind + 2]
            used = lane < (block[4:5] if kind == 0 else limit)
            owner = second >> shift
            inner = second & (leaves - 1)
            if rel is not None:
                line = 0 if kind == 0 else max(rel, 1)
                segments.append((line, inner, rel * leaves + first, used & (owner == me)))
                continue
            apart = jnp.bitwise_xor(owner, me)
            slot = apart * leaves + inner
            if kind == 0:
                segments.append((0, first, slot, used))
            else:
                segments.append((1, first, slot, used & (apart < 2)))
                segments.append((2, first, slot, used & (apart == 2)))
                segments.append((3, first, slot, used & (apart == 3)))
    masks = jnp.concatenate([jnp.where(part[3], 1.0, 0.0) for part in segments], 0)
    masks = jnp.concatenate([masks, jnp.zeros((-len(segments) % 16, skeleton), F32)], 0)
    before = lax.broadcasted_iota(jnp.int32, (skeleton, skeleton), 0) < lax.broadcasted_iota(
        jnp.int32, (skeleton, skeleton), 1
    )
    prefix = dot(masks.astype(BF16), jnp.where(before, 1.0, 0.0).astype(BF16), 1, 0)
    totals = jnp.sum(masks, axis=1, keepdims=True)
    width = lists.shape[1]
    for line in range(4):
        offset = jnp.zeros((1, 1), F32)
        result = jnp.zeros((8, width), F32)
        for index, part in enumerate(segments):
            if part[0] != line:
                continue
            place = jnp.where(part[3], prefix[index : index + 1] + offset, -1.0)
            offset += totals[index : index + 1]
            spots = lax.broadcasted_iota(jnp.int32, (width, skeleton), 0)
            hot = jnp.where(spots == place.astype(jnp.int32), 1.0, 0.0).astype(BF16)
            values = jnp.concatenate(
                [part[1].astype(F32), part[2].astype(F32), jnp.zeros((6, skeleton), F32)], 0
            ).astype(BF16)
            result += dot(values, hot, 1, 1)
        lists[2 * line : 2 * line + 2] = result[:2].astype(jnp.int32)
        lists[8 + line : 9 + line] = jnp.broadcast_to(offset, (1, width)).astype(jnp.int32)
    lists[12:] = jnp.zeros((4, width), jnp.int32)


def build(rel, points, q1, q2, rhs, rhs_c, sw):
    leaves = q2.shape[0]
    size = points.shape[2]
    base = rel * leaves
    skels = q1[q1.shape[0] - leaves :].astype(F32).astype(jnp.int32)
    for leaf in range(leaves):
        right = with_norms(points[leaf], False)
        rhs[base + leaf] = right
        rhs_c[base + leaf] = dot(right, one_hot(skels[leaf : leaf + 1], size), 1, 0).astype(BF16)
        sw[base + leaf] = q2[leaf]


def level_kernel(features, height, mine, other, basis, skel, after, node, pair):
    skeleton = mine.shape[1]
    on_right = (lax.axis_index("leaf") >> (height - 1)) & 1
    pair[0] = mine[...]
    pair[1] = other[...]
    left = pair[on_right]
    right = pair[1 - on_right]
    line = skel[0, height - 1 : height, :]
    weights = dot(left[features:], basis[0, height - 1, :, :skeleton], 1, 1)
    weights += dot(right[features:], basis[0, height - 1, :, skeleton:], 1, 1)
    coords = dot(left[:features], one_hot(line, skeleton), 1, 0)
    coords += dot(right[:features], one_hot(line, skeleton, skeleton), 1, 0)
    node[:features] = coords.astype(BF16)
    node[features:] = weights.astype(BF16)


def far_sums(line, size, lists, lhs_c, rhs_c, sw, far):
    skeleton = rhs_c.shape[2]
    count = lists[8 + line, 0]

    def some(start, many):
        results = []
        for index in range(0, many, 2):
            spots = [start + index + half for half in range(2)]
            owns = [lists[2 * line, spot] for spot in spots]
            slots = [lists[2 * line + 1, spot] for spot in spots]
            blocks = [tile(lhs_c[own], rhs_c[slot], 1, 0) for own, slot in zip(owns, slots)]
            weights = jnp.concatenate([sw[slot, :, size:] for slot in slots], 0)
            part = dot(weights, jnp.concatenate(blocks, 0), 1, 1)
            probes = part.shape[0] // 2
            for half in range(2):
                rows = slice(half * probes, (half + 1) * probes)
                mine = part[rows, half * skeleton : (half + 1) * skeleton]
                mine = mine.astype(BF16).astype(F32)
                results.append((owns[half], jnp.where(spots[half] < count, mine, 0.0)))
        for own, part in results:
            far[own] += part

    stepped(count, FAR_STEP, some)


def near_sums(size, lists, lhs_t, rhs, sw, near):
    count = lists[8, 0]

    def some(start, many):
        results = []
        for index in range(many):
            spot = start + index
            own, slot = lists[0, spot], lists[1, spot]
            block = tile(lhs_t[own], rhs[slot], 1, 0)
            part = dot(sw[slot, :, :size], block, 1, 1)
            results.append((own, jnp.where(spot < count, part, 0.0)))
        for own, part in results:
            near[own] += part

    stepped(count, NEAR_STEP, some)


def stepped(count, many, some):
    half = many // 2
    whole = (count + half - 1) // many

    def step_of(step, carry):
        some(step * many, many)
        return carry

    lax.fori_loop(0, whole, step_of, 0)

    @pl.when(count > whole * many)
    def _():
        some(whole * many, half)


def first_kernel(points, q1, q2, lists, lhs_c, _, __, ___, rhs, rhs_c, sw, far):
    build(1, points, q1, q2, rhs, rhs_c, sw)
    far[...] = jnp.zeros_like(far)
    far_sums(1, points.shape[2], lists, lhs_c, rhs_c, sw, far)


def other_kernel(
    rel, points, q1, q2, lists, lhs_c, after, _, __, ___, ____,
    rhs, rhs_c, sw, far,
):
    build(rel, points, q1, q2, rhs, rhs_c, sw)
    far_sums(rel, rhs.shape[2], lists, lhs_c, rhs_c, sw, far)


def last_kernel(features, levels, *refs):
    nodes, refs = refs[: 2 * levels], refs[2 * levels :]
    upper_basis, subtree_basis, dev_basis, leaf_basis, lists, lhs_t, rhs, sw, far, near, out = refs
    leaves, probes, size = out.shape
    skeleton = nodes[0].shape[1]
    me = lax.axis_index("sub")
    subtree = lax.axis_index("leaf")
    tree = []
    for level in range(levels):
        mine, other = nodes[2 * level], nodes[2 * level + 1]
        block = tile(
            with_norms(mine[:features], True), with_norms(other[:features], False), 0, 0
        )
        tree.append(dot(other[features:], block, 1, 1))
    potential = tree[levels - 1]
    for height in range(levels - 1, 0, -1):
        side = pl.multiple_of(((subtree >> (height - 1)) & 1) * skeleton, skeleton)
        part = upper_basis[0, height - 1, :, pl.ds(side, skeleton)]
        potential = tree[height - 1] + dot(potential.astype(BF16), part, 1, 0)
    spot = pl.multiple_of(me * skeleton, skeleton)
    device = dot(potential.astype(BF16), subtree_basis[0, :, pl.ds(spot, skeleton)], 1, 0)
    spread = dot(device.astype(BF16), dev_basis[0], 1, 0).astype(BF16)
    for leaf in range(leaves):
        total = spread[:, leaf * skeleton : (leaf + 1) * skeleton].astype(F32) + far[leaf]
        high = total.astype(BF16)
        low = (total - high.astype(F32)).astype(BF16)
        part = dot(jnp.concatenate([high, low], 0), leaf_basis[leaf], 1, 0)
        out[leaf] = near[leaf] + part[:probes] + part[probes:]
    near_sums(size, lists, lhs_t, rhs, sw, out)


def call(kernel, out_shape, in_specs, micros, *args, scratch=(), aliases=()):
    return pl.pallas_call(
        kernel,
        out_shape=out_shape,
        in_specs=in_specs,
        out_specs=jax.tree.map(lambda _: VMEM, out_shape),
        scratch_shapes=scratch,
        input_output_aliases=dict(aliases),
        compiler_params=pltpu.CompilerParams(vmem_limit_bytes=VMEM_LIMIT),
        cost_estimate=pl.CostEstimate(
            flops=int(micros * 1e9), bytes_accessed=int(micros * 1e6), transcendentals=0
        ),
    )(*args)


def placed(*arrays):
    return [pltpu.with_memory_space_constraint(array, pltpu.HBM) for array in arrays]


def on_device(
    points,
    probe_bits,
    leaf_skel,
    leaf_basis,
    device_skel,
    device_basis,
    subtree_skel,
    subtree_basis,
    upper_skel,
    upper_basis,
    near_pairs,
    near_count,
    far_pairs,
):
    leaves, features, size = points.shape
    probes = probe_bits.shape[1]
    skeleton = leaf_skel.shape[1]
    levels = lax.axis_size("leaf").bit_length() - 1
    cap = near_pairs.shape[1]
    far_cap = far_pairs.shape[1]
    depth = features + AUG
    width = max(-(-5 * cap // 128), -(-3 * far_cap // 128)) * 128
    q1_rows = features + probes + LIST_ROWS + leaves
    slots = 4 * leaves
    shape = jax.ShapeDtypeStruct
    rhs_shape = shape((slots, depth, size), BF16)
    rhs_c_shape = shape((slots, depth, skeleton), BF16)
    sw_shape = shape((slots, probes, size + skeleton), BF16)
    near_shape = shape((leaves, probes, size), F32)
    far_shape = shape((leaves, probes, skeleton), F32)
    node_shape = shape((features + probes, skeleton), BF16)
    token_shape = shape(TOKEN, F32)

    q1, q2 = call(
        prep_kernel,
        (shape((q1_rows, skeleton), BF16), shape((leaves, probes, size + skeleton), BF16)),
        [HBM] * 7 + [SMEM, HBM],
        4,
        *placed(points, probe_bits, leaf_skel, leaf_basis, device_skel, device_basis),
        *placed(jnp.swapaxes(near_pairs, 1, 2)),
        near_count,
        *placed(jnp.swapaxes(far_pairs, 1, 2)),
        scratch=[
            pltpu.VMEM(points.shape, BF16),
            pltpu.VMEM(probe_bits.shape, jnp.int32),
            pltpu.VMEM(leaf_skel.shape, jnp.int32),
            pltpu.VMEM(leaf_basis.shape, BF16),
            pltpu.VMEM(device_skel.shape, jnp.int32),
            pltpu.VMEM(device_basis.shape[1:], BF16),
            pltpu.VMEM((1, 2, cap), jnp.int32),
            pltpu.VMEM((1, 2, far_cap), jnp.int32),
            pltpu.SemaphoreType.DMA((4 + 4 * CHUNKS,)),
        ],
    )
    q1_one, q1_two, q1_three = (
        flipped(q1, "sub", bits) for bits in (1, 2, 3)
    )
    q2_two = flipped(q2, "sub", 2)
    points_two = flipped(points, "sub", 2)
    q2_one = flipped(q2, "sub", 1)
    points_one = flipped(points, "sub", 1)

    lhs_t, lhs_c, rhs, rhs_c, sw, near, token = call(
        own_kernel,
        (
            shape((leaves, size, depth), BF16),
            shape((leaves, skeleton, depth), BF16),
            rhs_shape,
            rhs_c_shape,
            sw_shape,
            near_shape,
            token_shape,
        ),
        [VMEM] * 3,
        5,
        points,
        leaf_skel,
        q2,
    )
    node, lists = call(
        functools.partial(node_kernel, features, probes, cap, far_cap),
        (node_shape, shape((16, width), jnp.int32)),
        [VMEM] * 6 + [ANY],
        2,
        q1,
        q1_one,
        q1_two,
        q1_three,
        subtree_basis,
        subtree_skel,
        token,
        scratch=[pltpu.VMEM((4, q1_rows, skeleton), BF16)],
    )
    nodes = []
    far = after = None
    for height in range(1, levels + 1):
        other = flipped(node, "leaf", 1 << (height - 1))
        nodes += [node, other]
        if height == 1:
            rhs, rhs_c, sw, far = call(
                first_kernel,
                (rhs_shape, rhs_c_shape, sw_shape, far_shape),
                [VMEM] * 3 + [SMEM, VMEM] + [ANY] * 3,
                5,
                points_one,
                q1_one,
                q2_one,
                lists,
                lhs_c,
                rhs,
                rhs_c,
                sw,
                aliases=((5, 0), (6, 1), (7, 2)),
            )
            after = far
        if height < levels:
            node = call(
                functools.partial(level_kernel, features, height),
                node_shape,
                [VMEM] * 4 + [ANY],
                1,
                node,
                other,
                upper_basis,
                upper_skel,
                after,
                scratch=[pltpu.VMEM((2, features + probes, skeleton), BF16)],
            )

    points_three = flipped(points_two, "sub", 1)
    q2_three = flipped(q2_two, "sub", 1)
    for rel, sources in (
        (2, (points_two, q1_two, q2_two)), (3, (points_three, q1_three, q2_three))
    ):
        rhs, rhs_c, sw, far = call(
            functools.partial(other_kernel, rel),
            (rhs_shape, rhs_c_shape, sw_shape, far_shape),
            [VMEM] * 3 + [SMEM, VMEM] + [ANY] * 4 + [VMEM],
            3,
            *sources,
            lists,
            lhs_c,
            node,
            rhs,
            rhs_c,
            sw,
            far,
            aliases=((6, 0), (7, 1), (8, 2), (9, 3)),
        )

    return call(
        functools.partial(last_kernel, features, levels),
        near_shape,
        [VMEM] * (2 * levels + 4) + [SMEM] + [VMEM] * 5,
        10,
        *nodes,
        upper_basis,
        subtree_basis,
        device_basis,
        leaf_basis,
        lists,
        lhs_t,
        rhs,
        sw,
        far,
        near,
    )


def solution(mesh):
    return jax.shard_map(
        on_device,
        mesh=mesh,
        in_specs=(
            P(("leaf", "sub"), None, None),
            P(("leaf", "sub"), None, None),
            P(("leaf", "sub"), None),
            P(("leaf", "sub"), None, None),
            P(("leaf", "sub"), None),
            P(("leaf", "sub"), None, None),
            P("leaf", None),
            P("leaf", None, None),
            P("leaf", None, None),
            P("leaf", None, None, None),
            P(("leaf", "sub"), None, None),
            P(("leaf", "sub")),
            P(("leaf", "sub"), None, None),
        ),
        out_specs=P(("leaf", "sub"), None, None),
        check_vma=False,
    )
```

```python
import functools

import jax
import jax.numpy as jnp
from jax import lax
from jax.experimental import pallas as pl
from jax.experimental.pallas import tpu as pltpu
from jax.sharding import PartitionSpec as P


BF16 = jnp.bfloat16
F32 = jnp.float32
AUG = 16
NEAR_STEP = 16
OWN_STEP = 8
CHUNKS = 4
FAR_STEP = 32
LIST_ROWS = 16
LINES = 5
PACK = 256
VMEM = pl.BlockSpec(memory_space=pltpu.VMEM)
SMEM = pl.BlockSpec(memory_space=pltpu.SMEM)
ANY = pl.BlockSpec(memory_space=pl.ANY)
HBM = pl.BlockSpec(memory_space=pltpu.HBM)
VMEM_LIMIT = 24 << 20
TOKEN = (8, 128)


def flipped(block, axis, bits):
    count = lax.axis_size(axis)
    return lax.ppermute(block, axis, [(low, low ^ bits) for low in range(count)])


def dot(left, right, left_dim, right_dim):
    return lax.dot_general(
        left, right, (((left_dim,), (right_dim,)), ((), ())), preferred_element_type=F32
    )


def one_hot(columns, rows, start=0):
    spots = lax.broadcasted_iota(jnp.int32, (rows, columns.shape[1]), 0) + start
    return jnp.where(spots == columns, 1.0, 0.0).astype(BF16)


def norm_parts(coords):
    wide = coords.astype(F32)
    norm = jnp.sum(wide * wide, axis=0, keepdims=True) * (-1.0 / coords.shape[0])
    high = norm.astype(BF16).astype(F32)
    rest = norm - high
    middle = rest.astype(BF16).astype(F32)
    return high, middle, rest - middle


def aug_rows(parts, width, norm_first):
    row = lax.broadcasted_iota(jnp.int32, (AUG, width), 0)
    start, ones = (0, 3) if norm_first else (3, 0)
    block = jnp.where((row >= ones) & (row < ones + 3), 1.0, 0.0)
    for index, part in enumerate(parts):
        block = jnp.where(row == start + index, part, block)
    return block.astype(BF16)


def with_norms(coords, norm_first):
    rows = aug_rows(norm_parts(coords), coords.shape[1], norm_first)
    scaled = (coords.astype(F32) * (2.0 / coords.shape[0])).astype(BF16) if norm_first else coords
    return jnp.concatenate([scaled, rows], axis=0)


def tile(left, right, left_dim, right_dim):
    return jnp.exp(dot(left, right, left_dim, right_dim)).astype(BF16)


def list_rows(pairs, row, width):
    pick = lax.broadcasted_iota(jnp.int32, (8, 2), 0) == lax.broadcasted_iota(
        jnp.int32, (8, 2), 1
    ) + row
    spread = jnp.where(pick, 1.0, 0.0).astype(BF16)
    rows = dot(spread, pairs.astype(F32).astype(BF16), 1, 0)
    short = width - pairs.shape[1]
    return jnp.concatenate([rows, jnp.zeros((8, short), F32)], axis=1) if short else rows


def prep_kernel(
    points_in, bits_in, skel_in, basis_in, dev_skel_in, dev_basis_in, near_in, near_count, far_in,
    q1, q2, points, bits, leaf_skel, leaf_basis, dev_skel, dev_basis, near, far, sems,
):
    leaves, features, size = points.shape
    probes = bits.shape[1]
    skeleton = leaf_skel.shape[1]
    small = [
        pltpu.make_async_copy(source, target, sems.at[index])
        for index, (source, target) in enumerate(
            ((skel_in, leaf_skel), (dev_skel_in, dev_skel), (near_in, near), (far_in, far))
        )
    ]
    chunk = leaves // CHUNKS
    large = []
    for index in range(CHUNKS):
        rows = pl.ds(index * chunk, chunk)
        columns = pl.ds(index * chunk * skeleton, chunk * skeleton)
        base = 4 + 4 * index
        large.append(
            [
                pltpu.make_async_copy(points_in.at[rows], points.at[rows], sems.at[base]),
                pltpu.make_async_copy(bits_in.at[rows], bits.at[rows], sems.at[base + 1]),
                pltpu.make_async_copy(basis_in.at[rows], leaf_basis.at[rows], sems.at[base + 2]),
                pltpu.make_async_copy(
                    dev_basis_in.at[0, :, columns], dev_basis.at[:, columns], sems.at[base + 3]
                ),
            ]
        )
    for copy in small + [copy for group in large for copy in group]:
        copy.start()
    for copy in small:
        copy.wait()
    names = jnp.concatenate(
        [leaf_skel[...].astype(F32), jnp.broadcast_to(dev_skel[...].astype(F32), (8, skeleton))], 0
    ).T
    lane = lax.broadcasted_iota(jnp.int32, (skeleton, size), 1).astype(F32)
    total = jnp.zeros((features + probes, size), F32)
    for first in range(0, leaves, 2):
        if first % chunk == 0:
            for copy in large[first // chunk]:
                copy.wait()
        coords, weights = [], []
        for leaf in (first, first + 1):
            signs = (2 * bits[leaf] - 1).astype(F32).astype(BF16)
            hot = jnp.where(lane == names[:, leaf : leaf + 1], 1.0, 0.0).astype(BF16)
            both = dot(
                jnp.concatenate([points[leaf], signs], 0),
                jnp.concatenate([hot, leaf_basis[leaf]], 0),
                1,
                1,
            ).astype(BF16)
            coords.append(both[:features, :skeleton])
            weights.append(both[features:, skeleton:])
            q2[leaf, :, :size] = signs
            q2[leaf, :, size:] = weights[-1]
        spots = lane + float(first * skeleton)
        hot = jnp.where(spots == names[:, leaves : leaves + 1], 1.0, 0.0).astype(BF16)
        columns = slice(first * skeleton, (first + 2) * skeleton)
        total += dot(
            jnp.concatenate([jnp.concatenate(coords, 1), jnp.concatenate(weights, 1)], 0),
            jnp.concatenate([hot, dev_basis[:, columns]], 0),
            1,
            1,
        )
    q1[:features] = total[:features, :skeleton].astype(BF16)
    q1[features : features + probes] = total[features:, skeleton:].astype(BF16)
    lists = list_rows(near[0], 0, skeleton) + list_rows(far[0], 2, skeleton)
    row = lax.broadcasted_iota(jnp.int32, lists.shape, 0)
    lists = jnp.where(row == 4, near_count[0].astype(F32), lists)
    base = features + probes
    q1[base : base + LIST_ROWS] = jnp.concatenate([lists, jnp.zeros_like(lists)], 0).astype(BF16)
    q1[base + LIST_ROWS :] = leaf_skel[...].astype(F32).astype(BF16)


def own_kernel(points, leaf_skel, q2, lhs_t, lhs_c, rhs, rhs_c, sw, near, token):
    leaves, features, size = points.shape
    for leaf in range(leaves):
        left = with_norms(points[leaf], True)
        right = with_norms(points[leaf], False)
        both = dot(
            jnp.concatenate([left, right], 0), one_hot(leaf_skel[leaf : leaf + 1, :], size), 1, 0
        ).astype(BF16)
        rhs[leaf] = right
        lhs_t[leaf] = left.T
        lhs_c[leaf] = both[: features + AUG].T
        rhs_c[leaf] = both[features + AUG :]
        sw[leaf] = q2[leaf]

    def step_of(step, carry):
        for index in range(OWN_STEP):
            leaf = step * OWN_STEP + index
            block = tile(lhs_t[leaf], rhs[leaf], 1, 0)
            near[leaf] = dot(q2[leaf, :, :size], block, 1, 1)
        return carry

    lax.fori_loop(0, leaves // OWN_STEP, step_of, 0)
    token[...] = jnp.zeros_like(token)


def node_kernel(
    features, probes, cap, far_cap, mine, one, two, three, basis, skel, token, node, lists, q1
):
    skeleton = mine.shape[1]
    leaves = mine.shape[0] - features - probes - LIST_ROWS
    shift = leaves.bit_length() - 1
    groups = 4
    me = lax.axis_index("sub")
    for rel, ref in enumerate((mine, one, two, three)):
        q1[rel] = ref[...]
    weights = jnp.zeros((probes, skeleton), F32)
    coords = jnp.zeros((features, skeleton), F32)
    for spot in range(groups):
        block = q1[jnp.bitwise_xor(me, spot)]
        span = slice(spot * skeleton, (spot + 1) * skeleton)
        weights += dot(block[features : features + probes], basis[0, :, span], 1, 1)
        coords += dot(block[:features], one_hot(skel[...], skeleton, spot * skeleton), 1, 0)
    node[:features] = coords.astype(BF16)
    node[features:] = weights.astype(BF16)

    base = features + probes
    lane = lax.broadcasted_iota(jnp.int32, (1, skeleton), 1)
    rows = [q1[rel, base : base + LIST_ROWS].astype(F32) for rel in range(groups)]
    whole = [block.astype(jnp.int32) for block in rows]
    segments = []
    for kind, limit in ((0, cap), (2, far_cap)):
        for rel in (None, 0, 1, 2, 3):
            block = whole[0 if rel is None else rel]
            first = block[kind : kind + 1]
            second = block[kind + 1 : kind + 2]
            used = lane < (block[4:5] if kind == 0 else limit)
            owner = second >> shift
            inner = second & (leaves - 1)
            if rel is not None:
                line = rel >> 1 if kind == 0 else 1 + max(rel, 1)
                segments.append((line, inner, rel * leaves + first, used & (owner == me)))
                continue
            apart = jnp.bitwise_xor(owner, me)
            slot = apart * leaves + inner
            if kind == 0:
                segments.append((0, first, slot, used & (apart < 2)))
                segments.append((1, first, slot, used & (apart >= 2)))
            else:
                segments.append((2, first, slot, used & (apart < 2)))
                segments.append((3, first, slot, used & (apart == 2)))
                segments.append((4, first, slot, used & (apart == 3)))
    masks = jnp.concatenate([jnp.where(part[3], 1.0, 0.0) for part in segments], 0)
    masks = jnp.concatenate([masks, jnp.zeros((-len(segments) % 16, skeleton), F32)], 0)
    before = lax.broadcasted_iota(jnp.int32, (skeleton, skeleton), 0) < lax.broadcasted_iota(
        jnp.int32, (skeleton, skeleton), 1
    )
    prefix = dot(masks.astype(BF16), jnp.where(before, 1.0, 0.0).astype(BF16), 1, 0)
    totals = jnp.sum(masks, axis=1, keepdims=True)
    width = lists.shape[1]
    counts = jnp.zeros((1, skeleton), F32)
    for line in range(LINES):
        offset = jnp.zeros((1, 1), F32)
        result = jnp.zeros((8, width), F32)
        for index, part in enumerate(segments):
            if part[0] != line:
                continue
            place = jnp.where(part[3], prefix[index : index + 1] + offset, -1.0)
            offset += totals[index : index + 1]
            spots = lax.broadcasted_iota(jnp.int32, (width, skeleton), 0)
            hot = jnp.where(spots == place.astype(jnp.int32), 1.0, 0.0).astype(BF16)
            values = jnp.concatenate(
                [part[1].astype(F32), part[2].astype(F32), jnp.zeros((6, skeleton), F32)], 0
            ).astype(BF16)
            result += dot(values, hot, 1, 1)
        whole_result = result.astype(jnp.int32)
        lists[line : line + 1] = whole_result[:1] + whole_result[1:2] * PACK
        counts = jnp.where(lane == line, jnp.broadcast_to(offset, (1, skeleton)), counts)
    lists[LINES : LINES + 1, :skeleton] = counts.astype(jnp.int32)
    lists[LINES : LINES + 1, skeleton:] = jnp.zeros((1, width - skeleton), jnp.int32)
    lists[LINES + 1 :] = jnp.zeros((8 - LINES - 1, width), jnp.int32)


def build(rel, points, q1, q2, rhs, rhs_c, sw):
    leaves = q2.shape[0]
    size = points.shape[2]
    base = rel * leaves
    skels = q1[q1.shape[0] - leaves :].astype(F32).astype(jnp.int32)
    for leaf in range(leaves):
        right = with_norms(points[leaf], False)
        rhs[base + leaf] = right
        rhs_c[base + leaf] = dot(right, one_hot(skels[leaf : leaf + 1], size), 1, 0).astype(BF16)
        sw[base + leaf] = q2[leaf]


def level_kernel(features, height, mine, other, basis, skel, after, node, pair):
    skeleton = mine.shape[1]
    on_right = (lax.axis_index("leaf") >> (height - 1)) & 1
    pair[0] = mine[...]
    pair[1] = other[...]
    left = pair[on_right]
    right = pair[1 - on_right]
    line = skel[0, height - 1 : height, :]
    weights = dot(left[features:], basis[0, height - 1, :, :skeleton], 1, 1)
    weights += dot(right[features:], basis[0, height - 1, :, skeleton:], 1, 1)
    coords = dot(left[:features], one_hot(line, skeleton), 1, 0)
    coords += dot(right[:features], one_hot(line, skeleton, skeleton), 1, 0)
    node[:features] = coords.astype(BF16)
    node[features:] = weights.astype(BF16)


def entry(lists, line, spot):
    value = lists[line, spot]
    return value & (PACK - 1), value // PACK


def far_sums(line, size, lists, lhs_c, rhs_c, sw, far):
    skeleton = rhs_c.shape[2]
    count = lists[LINES, line]

    def some(start, many):
        results = []
        for index in range(0, many, 2):
            spots = [start + index + half for half in range(2)]
            owns, slots = zip(*[entry(lists, line, spot) for spot in spots])
            blocks = [tile(lhs_c[own], rhs_c[slot], 1, 0) for own, slot in zip(owns, slots)]
            weights = jnp.concatenate([sw[slot, :, size:] for slot in slots], 0)
            part = dot(weights, jnp.concatenate(blocks, 0), 1, 1)
            probes = part.shape[0] // 2
            for half in range(2):
                rows = slice(half * probes, (half + 1) * probes)
                mine = part[rows, half * skeleton : (half + 1) * skeleton]
                mine = mine.astype(BF16).astype(F32)
                results.append((owns[half], jnp.where(spots[half] < count, mine, 0.0)))
        for own, part in results:
            far[own] += part

    stepped(count, FAR_STEP, some)


def near_parts(line, start, many, size, lists, lhs_t, rhs, sw):
    count = lists[LINES, line]
    results = []
    for index in range(many):
        spot = start + index
        own, slot = entry(lists, line, spot)
        block = tile(lhs_t[own], rhs[slot], 1, 0)
        part = dot(sw[slot, :, :size], block, 1, 1)
        results.append((own, jnp.where(spot < count, part, 0.0)))
    return results


def near_sums(line, size, lists, lhs_t, rhs, sw, near, done=0):
    def some(start, many):
        for own, part in near_parts(line, start + done, many, size, lists, lhs_t, rhs, sw):
            near[own] += part

    stepped(lists[LINES, line] - done, NEAR_STEP, some)


def stepped(count, many, some):
    half = many // 2
    whole = jnp.maximum(count + half - 1, 0) // many

    def step_of(step, carry):
        some(step * many, many)
        return carry

    lax.fori_loop(0, whole, step_of, 0)

    @pl.when(count > whole * many)
    def _():
        some(whole * many, half)


def first_kernel(points, q1, q2, lists_in, lhs_c, _, __, ___, rhs, rhs_c, sw, far, lists, sem):
    copy = pltpu.make_async_copy(lists_in, lists, sem)
    copy.start()
    build(1, points, q1, q2, rhs, rhs_c, sw)
    far[...] = jnp.zeros_like(far)
    copy.wait()
    far_sums(2, points.shape[2], lists, lhs_c, rhs_c, sw, far)


def other_kernel(
    rel, points, q1, q2, lists_in, lhs_c, after, _, __, ___, ____,
    rhs, rhs_c, sw, far, lists, sem,
):
    copy = pltpu.make_async_copy(lists_in, lists, sem)
    copy.start()
    build(rel, points, q1, q2, rhs, rhs_c, sw)
    copy.wait()
    far_sums(rel + 1, rhs.shape[2], lists, lhs_c, rhs_c, sw, far)


def mid_kernel(size, lists_in, lhs_t, rhs, sw, near_in, _, near, lists, sem):
    copy = pltpu.make_async_copy(lists_in, lists, sem)
    copy.start()
    copy.wait()
    near_sums(0, size, lists, lhs_t, rhs, sw, near)


def last_kernel(features, levels, *refs):
    nodes, refs = refs[: 2 * levels], refs[2 * levels :]
    upper_basis, subtree_basis, dev_basis, leaf_basis, lists_in, lhs_t, *refs = refs
    rhs, sw, far, near, out, lists, sem = refs
    copy = pltpu.make_async_copy(lists_in, lists, sem)
    copy.start()
    leaves, probes, size = out.shape
    skeleton = nodes[0].shape[1]
    me = lax.axis_index("sub")
    subtree = lax.axis_index("leaf")
    tree = []
    for level in range(levels):
        mine, other = nodes[2 * level], nodes[2 * level + 1]
        block = tile(
            with_norms(mine[:features], True), with_norms(other[:features], False), 0, 0
        )
        tree.append(dot(other[features:], block, 1, 1))
    potential = tree[levels - 1]
    for height in range(levels - 1, 0, -1):
        side = pl.multiple_of(((subtree >> (height - 1)) & 1) * skeleton, skeleton)
        part = upper_basis[0, height - 1, :, pl.ds(side, skeleton)]
        potential = tree[height - 1] + dot(potential.astype(BF16), part, 1, 0)
    spot = pl.multiple_of(me * skeleton, skeleton)
    device = dot(potential.astype(BF16), subtree_basis[0, :, pl.ds(spot, skeleton)], 1, 0)
    spread = dot(device.astype(BF16), dev_basis[0], 1, 0).astype(BF16)
    copy.wait()
    early = near_parts(1, 0, NEAR_STEP // 2, size, lists, lhs_t, rhs, sw)
    for leaf in range(leaves):
        total = spread[:, leaf * skeleton : (leaf + 1) * skeleton].astype(F32) + far[leaf]
        high = total.astype(BF16)
        low = (total - high.astype(F32)).astype(BF16)
        part = dot(jnp.concatenate([high, low], 0), leaf_basis[leaf], 1, 0)
        out[leaf] = near[leaf] + part[:probes] + part[probes:]
    for own, part in early:
        out[own] += part
    near_sums(1, size, lists, lhs_t, rhs, sw, out, NEAR_STEP // 2)


def call(kernel, out_shape, in_specs, micros, *args, scratch=(), aliases=(), out_specs=None):
    return pl.pallas_call(
        kernel,
        out_shape=out_shape,
        in_specs=in_specs,
        out_specs=out_specs or jax.tree.map(lambda _: VMEM, out_shape),
        scratch_shapes=scratch,
        input_output_aliases=dict(aliases),
        compiler_params=pltpu.CompilerParams(vmem_limit_bytes=VMEM_LIMIT),
        cost_estimate=pl.CostEstimate(
            flops=int(micros * 1e9), bytes_accessed=int(micros * 1e6), transcendentals=0
        ),
    )(*args)


def placed(*arrays):
    return [pltpu.with_memory_space_constraint(array, pltpu.HBM) for array in arrays]


def on_device(
    points,
    probe_bits,
    leaf_skel,
    leaf_basis,
    device_skel,
    device_basis,
    subtree_skel,
    subtree_basis,
    upper_skel,
    upper_basis,
    near_pairs,
    near_count,
    far_pairs,
):
    leaves, features, size = points.shape
    probes = probe_bits.shape[1]
    skeleton = leaf_skel.shape[1]
    levels = lax.axis_size("leaf").bit_length() - 1
    cap = near_pairs.shape[1]
    far_cap = far_pairs.shape[1]
    depth = features + AUG
    width = max(-(-3 * cap // 128), -(-3 * far_cap // 128)) * 128
    q1_rows = features + probes + LIST_ROWS + leaves
    slots = 4 * leaves
    shape = jax.ShapeDtypeStruct
    rhs_shape = shape((slots, depth, size), BF16)
    rhs_c_shape = shape((slots, depth, skeleton), BF16)
    sw_shape = shape((slots, probes, size + skeleton), BF16)
    near_shape = shape((leaves, probes, size), F32)
    far_shape = shape((leaves, probes, skeleton), F32)
    node_shape = shape((features + probes, skeleton), BF16)
    token_shape = shape(TOKEN, F32)
    line_scratch = [pltpu.SMEM((8, width), jnp.int32), pltpu.SemaphoreType.DMA]

    q1, q2 = call(
        prep_kernel,
        (shape((q1_rows, skeleton), BF16), shape((leaves, probes, size + skeleton), BF16)),
        [HBM] * 7 + [SMEM, HBM],
        4,
        *placed(points, probe_bits, leaf_skel, leaf_basis, device_skel, device_basis),
        *placed(jnp.swapaxes(near_pairs, 1, 2)),
        near_count,
        *placed(jnp.swapaxes(far_pairs, 1, 2)),
        scratch=[
            pltpu.VMEM(points.shape, BF16),
            pltpu.VMEM(probe_bits.shape, jnp.int32),
            pltpu.VMEM(leaf_skel.shape, jnp.int32),
            pltpu.VMEM(leaf_basis.shape, BF16),
            pltpu.VMEM(device_skel.shape, jnp.int32),
            pltpu.VMEM(device_basis.shape[1:], BF16),
            pltpu.VMEM((1, 2, cap), jnp.int32),
            pltpu.VMEM((1, 2, far_cap), jnp.int32),
            pltpu.SemaphoreType.DMA((4 + 4 * CHUNKS,)),
        ],
    )
    q1_one, q1_two, q1_three = (
        flipped(q1, "sub", bits) for bits in (1, 2, 3)
    )
    q2_two = flipped(q2, "sub", 2)
    points_two = flipped(points, "sub", 2)
    q2_one = flipped(q2, "sub", 1)
    points_one = flipped(points, "sub", 1)

    lhs_t, lhs_c, rhs, rhs_c, sw, near, token = call(
        own_kernel,
        (
            shape((leaves, size, depth), BF16),
            shape((leaves, skeleton, depth), BF16),
            rhs_shape,
            rhs_c_shape,
            sw_shape,
            near_shape,
            token_shape,
        ),
        [VMEM] * 3,
        5,
        points,
        leaf_skel,
        q2,
    )
    node, lists = call(
        functools.partial(node_kernel, features, probes, cap, far_cap),
        (node_shape, shape((8, width), jnp.int32)),
        [VMEM] * 6 + [ANY],
        2,
        q1,
        q1_one,
        q1_two,
        q1_three,
        subtree_basis,
        subtree_skel,
        token,
        scratch=[pltpu.VMEM((4, q1_rows, skeleton), BF16)],
    )
    nodes = []
    far = after = None
    for height in range(1, levels + 1):
        other = flipped(node, "leaf", 1 << (height - 1))
        nodes += [node, other]
        if height == 1:
            rhs, rhs_c, sw, far = call(
                first_kernel,
                (rhs_shape, rhs_c_shape, sw_shape, far_shape),
                [VMEM] * 3 + [ANY, VMEM] + [ANY] * 3,
                5,
                points_one,
                q1_one,
                q2_one,
                lists,
                lhs_c,
                rhs,
                rhs_c,
                sw,
                aliases=((5, 0), (6, 1), (7, 2)),
                scratch=line_scratch,
            )
            after = far
        if height < levels:
            node = call(
                functools.partial(level_kernel, features, height),
                node_shape,
                [VMEM] * 4 + [ANY],
                1,
                node,
                other,
                upper_basis,
                upper_skel,
                after,
                scratch=[pltpu.VMEM((2, features + probes, skeleton), BF16)],
            )

    near = call(
        functools.partial(mid_kernel, size),
        near_shape,
        [ANY] + [VMEM] * 4 + [ANY],
        5,
        lists,
        lhs_t,
        rhs,
        sw,
        near,
        node,
        aliases=((4, 0),),
        scratch=line_scratch,
    )
    points_three = flipped(points_two, "sub", 1)
    q2_three = flipped(q2_two, "sub", 1)
    for rel, sources in (
        (2, (points_two, q1_two, q2_two)), (3, (points_three, q1_three, q2_three))
    ):
        rhs, rhs_c, sw, far = call(
            functools.partial(other_kernel, rel),
            (rhs_shape, rhs_c_shape, sw_shape, far_shape),
            [VMEM] * 3 + [ANY, VMEM] + [ANY] * 4 + [VMEM],
            3,
            *sources,
            lists,
            lhs_c,
            node,
            rhs,
            rhs_c,
            sw,
            far,
            aliases=((6, 0), (7, 1), (8, 2), (9, 3)),
            scratch=line_scratch,
        )

    return call(
        functools.partial(last_kernel, features, levels),
        near_shape,
        [VMEM] * (2 * levels + 4) + [ANY] + [VMEM] * 5,
        10,
        *nodes,
        upper_basis,
        subtree_basis,
        device_basis,
        leaf_basis,
        lists,
        lhs_t,
        rhs,
        sw,
        far,
        near,
        scratch=line_scratch,
    )


def solution(mesh):
    return jax.shard_map(
        on_device,
        mesh=mesh,
        in_specs=(
            P(("leaf", "sub"), None, None),
            P(("leaf", "sub"), None, None),
            P(("leaf", "sub"), None),
            P(("leaf", "sub"), None, None),
            P(("leaf", "sub"), None),
            P(("leaf", "sub"), None, None),
            P("leaf", None),
            P("leaf", None, None),
            P("leaf", None, None),
            P("leaf", None, None, None),
            P(("leaf", "sub"), None, None),
            P(("leaf", "sub")),
            P(("leaf", "sub"), None, None),
        ),
        out_specs=P(("leaf", "sub"), None, None),
        check_vma=False,
    )
```

```python
import functools

import jax
import jax.numpy as jnp
from jax import lax
from jax.experimental import pallas as pl
from jax.experimental.pallas import tpu as pltpu
from jax.sharding import PartitionSpec as P


BF16 = jnp.bfloat16
F32 = jnp.float32
AUG = 16
NEAR_STEP = 16
OWN_STEP = 8
CHUNKS = 4
FAR_STEP = 32
LIST_ROWS = 16
LINES = 5
PACK = 256
VMEM = pl.BlockSpec(memory_space=pltpu.VMEM)
SMEM = pl.BlockSpec(memory_space=pltpu.SMEM)
ANY = pl.BlockSpec(memory_space=pl.ANY)
HBM = pl.BlockSpec(memory_space=pltpu.HBM)
VMEM_LIMIT = 24 << 20
TOKEN = (8, 128)


def flipped(block, axis, bits):
    count = lax.axis_size(axis)
    return lax.ppermute(block, axis, [(low, low ^ bits) for low in range(count)])


def dot(left, right, left_dim, right_dim):
    return lax.dot_general(
        left, right, (((left_dim,), (right_dim,)), ((), ())), preferred_element_type=F32
    )


def one_hot(columns, rows, start=0):
    spots = lax.broadcasted_iota(jnp.int32, (rows, columns.shape[1]), 0) + start
    return jnp.where(spots == columns, 1.0, 0.0).astype(BF16)


def norm_parts(coords):
    wide = coords.astype(F32)
    norm = jnp.sum(wide * wide, axis=0, keepdims=True) * (-1.0 / coords.shape[0])
    high = norm.astype(BF16).astype(F32)
    rest = norm - high
    middle = rest.astype(BF16).astype(F32)
    return high, middle, rest - middle


def aug_rows(parts, width, norm_first):
    row = lax.broadcasted_iota(jnp.int32, (AUG, width), 0)
    start, ones = (0, 3) if norm_first else (3, 0)
    block = jnp.where((row >= ones) & (row < ones + 3), 1.0, 0.0)
    for index, part in enumerate(parts):
        block = jnp.where(row == start + index, part, block)
    return block.astype(BF16)


def with_norms(coords, norm_first):
    rows = aug_rows(norm_parts(coords), coords.shape[1], norm_first)
    scaled = (coords.astype(F32) * (2.0 / coords.shape[0])).astype(BF16) if norm_first else coords
    return jnp.concatenate([scaled, rows], axis=0)


def tile(left, right, left_dim, right_dim):
    return jnp.exp(dot(left, right, left_dim, right_dim)).astype(BF16)


def parts_of(pack, leaf, leaves, features, probes):
    size = pack.shape[1]
    skeleton = size // 2
    signs = leaves * features + leaf * probes
    weights = leaves * (features + probes) + (leaf // 2) * probes
    side = (leaf % 2) * skeleton
    return (
        pack.at[leaf * features : (leaf + 1) * features],
        pack.at[signs : signs + probes],
        pack.at[weights : weights + probes, side : side + skeleton],
    )


def list_rows(pairs, row, width):
    pick = lax.broadcasted_iota(jnp.int32, (8, 2), 0) == lax.broadcasted_iota(
        jnp.int32, (8, 2), 1
    ) + row
    spread = jnp.where(pick, 1.0, 0.0).astype(BF16)
    rows = dot(spread, pairs.astype(F32).astype(BF16), 1, 0)
    short = width - pairs.shape[1]
    return jnp.concatenate([rows, jnp.zeros((8, short), F32)], axis=1) if short else rows


def prep_kernel(
    points_in, bits_in, skel_in, basis_in, dev_skel_in, dev_basis_in, near_in, near_count, far_in,
    q1, q2, points, bits, leaf_skel, leaf_basis, dev_skel, dev_basis, near, far, sems,
):
    leaves, features, size = points.shape
    probes = bits.shape[1]
    skeleton = leaf_skel.shape[1]
    small = [
        pltpu.make_async_copy(source, target, sems.at[index])
        for index, (source, target) in enumerate(
            ((skel_in, leaf_skel), (dev_skel_in, dev_skel), (near_in, near), (far_in, far))
        )
    ]
    chunk = leaves // CHUNKS
    large = []
    for index in range(CHUNKS):
        rows = pl.ds(index * chunk, chunk)
        columns = pl.ds(index * chunk * skeleton, chunk * skeleton)
        base = 4 + 4 * index
        large.append(
            [
                pltpu.make_async_copy(points_in.at[rows], points.at[rows], sems.at[base]),
                pltpu.make_async_copy(bits_in.at[rows], bits.at[rows], sems.at[base + 1]),
                pltpu.make_async_copy(basis_in.at[rows], leaf_basis.at[rows], sems.at[base + 2]),
                pltpu.make_async_copy(
                    dev_basis_in.at[0, :, columns], dev_basis.at[:, columns], sems.at[base + 3]
                ),
            ]
        )
    for copy in small + [copy for group in large for copy in group]:
        copy.start()
    for copy in small:
        copy.wait()
    lists = list_rows(near[0], 0, skeleton) + list_rows(far[0], 2, skeleton)
    row = lax.broadcasted_iota(jnp.int32, lists.shape, 0)
    lists = jnp.where(row == 4, near_count[0].astype(F32), lists)
    base = features + probes
    q1[base : base + LIST_ROWS] = jnp.concatenate([lists, jnp.zeros_like(lists)], 0).astype(BF16)
    q1[base + LIST_ROWS :] = leaf_skel[...].astype(F32).astype(BF16)
    names = jnp.concatenate(
        [leaf_skel[...].astype(F32), jnp.broadcast_to(dev_skel[...].astype(F32), (8, skeleton))], 0
    ).T
    lane = lax.broadcasted_iota(jnp.int32, (skeleton, size), 1).astype(F32)
    total = jnp.zeros((features + probes, size), F32)
    for first in range(0, leaves, 2):
        if first % chunk == 0:
            for copy in large[first // chunk]:
                copy.wait()
        coords, weights = [], []
        for leaf in (first, first + 1):
            signs = (2 * bits[leaf] - 1).astype(F32).astype(BF16)
            hot = jnp.where(lane == names[:, leaf : leaf + 1], 1.0, 0.0).astype(BF16)
            both = dot(
                jnp.concatenate([points[leaf], signs], 0),
                jnp.concatenate([hot, leaf_basis[leaf]], 0),
                1,
                1,
            ).astype(BF16)
            coords.append(both[:features, :skeleton])
            weights.append(both[features:, skeleton:])
            pack_points, pack_signs, pack_weights = parts_of(q2, leaf, leaves, features, probes)
            pack_points[...] = points[leaf]
            pack_signs[...] = signs
            pack_weights[...] = weights[-1]
        spots = lane + float(first * skeleton)
        hot = jnp.where(spots == names[:, leaves : leaves + 1], 1.0, 0.0).astype(BF16)
        columns = slice(first * skeleton, (first + 2) * skeleton)
        total += dot(
            jnp.concatenate([jnp.concatenate(coords, 1), jnp.concatenate(weights, 1)], 0),
            jnp.concatenate([hot, dev_basis[:, columns]], 0),
            1,
            1,
        )
    q1[:features] = total[:features, :skeleton].astype(BF16)
    q1[features : features + probes] = total[features:, skeleton:].astype(BF16)


def own_kernel(features, leaf_skel, q2, lhs_t, lhs_c, rhs, rhs_c, sw, near, token):
    leaves, probes, size = near.shape
    for leaf in range(leaves):
        points, signs, weights = parts_of(q2, leaf, leaves, features, probes)
        left = with_norms(points[...], True)
        right = with_norms(points[...], False)
        both = dot(
            jnp.concatenate([left, right], 0), one_hot(leaf_skel[leaf : leaf + 1, :], size), 1, 0
        ).astype(BF16)
        rhs[leaf] = right
        lhs_t[leaf] = left.T
        lhs_c[leaf] = both[: features + AUG].T
        rhs_c[leaf] = both[features + AUG :]
        sw[leaf, :, :size] = signs[...]
        sw[leaf, :, size:] = weights[...]

    def step_of(step, carry):
        for index in range(OWN_STEP):
            leaf = step * OWN_STEP + index
            block = tile(lhs_t[leaf], rhs[leaf], 1, 0)
            near[leaf] = dot(sw[leaf, :, :size], block, 1, 1)
        return carry

    lax.fori_loop(0, leaves // OWN_STEP, step_of, 0)
    token[...] = jnp.zeros_like(token)


def node_kernel(
    features, probes, cap, far_cap, mine, one, two, three, basis, skel, token, node, lists, q1
):
    skeleton = mine.shape[1]
    leaves = mine.shape[0] - features - probes - LIST_ROWS
    shift = leaves.bit_length() - 1
    groups = 4
    me = lax.axis_index("sub")
    for rel, ref in enumerate((mine, one, two, three)):
        q1[rel] = ref[...]
    weights = jnp.zeros((probes, skeleton), F32)
    coords = jnp.zeros((features, skeleton), F32)
    for spot in range(groups):
        block = q1[jnp.bitwise_xor(me, spot)]
        span = slice(spot * skeleton, (spot + 1) * skeleton)
        weights += dot(block[features : features + probes], basis[0, :, span], 1, 1)
        coords += dot(block[:features], one_hot(skel[...], skeleton, spot * skeleton), 1, 0)
    node[:features] = coords.astype(BF16)
    node[features:] = weights.astype(BF16)

    base = features + probes
    lane = lax.broadcasted_iota(jnp.int32, (1, skeleton), 1)
    rows = [q1[rel, base : base + LIST_ROWS].astype(F32) for rel in range(groups)]
    whole = [block.astype(jnp.int32) for block in rows]
    segments = []
    for kind, limit in ((0, cap), (2, far_cap)):
        for rel in (None, 0, 1, 2, 3):
            block = whole[0 if rel is None else rel]
            first = block[kind : kind + 1]
            second = block[kind + 1 : kind + 2]
            used = lane < (block[4:5] if kind == 0 else limit)
            owner = second >> shift
            inner = second & (leaves - 1)
            if rel is not None:
                line = rel >> 1 if kind == 0 else 1 + max(rel, 1)
                segments.append((line, inner, rel * leaves + first, used & (owner == me)))
                continue
            apart = jnp.bitwise_xor(owner, me)
            slot = apart * leaves + inner
            if kind == 0:
                segments.append((0, first, slot, used & (apart < 2)))
                segments.append((1, first, slot, used & (apart >= 2)))
            else:
                segments.append((2, first, slot, used & (apart < 2)))
                segments.append((3, first, slot, used & (apart == 2)))
                segments.append((4, first, slot, used & (apart == 3)))
    masks = jnp.concatenate([jnp.where(part[3], 1.0, 0.0) for part in segments], 0)
    masks = jnp.concatenate([masks, jnp.zeros((-len(segments) % 16, skeleton), F32)], 0)
    before = lax.broadcasted_iota(jnp.int32, (skeleton, skeleton), 0) < lax.broadcasted_iota(
        jnp.int32, (skeleton, skeleton), 1
    )
    prefix = dot(masks.astype(BF16), jnp.where(before, 1.0, 0.0).astype(BF16), 1, 0)
    totals = jnp.sum(masks, axis=1, keepdims=True)
    width = lists.shape[1]
    counts = jnp.zeros((1, skeleton), F32)
    for line in range(LINES):
        offset = jnp.zeros((1, 1), F32)
        result = jnp.zeros((8, width), F32)
        for index, part in enumerate(segments):
            if part[0] != line:
                continue
            place = jnp.where(part[3], prefix[index : index + 1] + offset, -1.0)
            offset += totals[index : index + 1]
            spots = lax.broadcasted_iota(jnp.int32, (width, skeleton), 0)
            hot = jnp.where(spots == place.astype(jnp.int32), 1.0, 0.0).astype(BF16)
            values = jnp.concatenate(
                [part[1].astype(F32), part[2].astype(F32), jnp.zeros((6, skeleton), F32)], 0
            ).astype(BF16)
            result += dot(values, hot, 1, 1)
        whole_result = result.astype(jnp.int32)
        lists[line : line + 1] = whole_result[:1] + whole_result[1:2] * PACK
        counts = jnp.where(lane == line, jnp.broadcast_to(offset, (1, skeleton)), counts)
    lists[LINES : LINES + 1, :skeleton] = counts.astype(jnp.int32)
    lists[LINES : LINES + 1, skeleton:] = jnp.zeros((1, width - skeleton), jnp.int32)
    lists[LINES + 1 :] = jnp.zeros((8 - LINES - 1, width), jnp.int32)


def build(rel, features, q1, q2, rhs, rhs_c, sw):
    probes, size = sw.shape[1], rhs.shape[2]
    leaves = rhs.shape[0] // 4
    base = rel * leaves
    skels = q1[q1.shape[0] - leaves :].astype(F32).astype(jnp.int32)
    for leaf in range(leaves):
        points, signs, weights = parts_of(q2, leaf, leaves, features, probes)
        right = with_norms(points[...], False)
        rhs[base + leaf] = right
        rhs_c[base + leaf] = dot(right, one_hot(skels[leaf : leaf + 1], size), 1, 0).astype(BF16)
        sw[base + leaf, :, :size] = signs[...]
        sw[base + leaf, :, size:] = weights[...]


def level_kernel(features, height, mine, other, basis, skel, after, node, pair):
    skeleton = mine.shape[1]
    on_right = (lax.axis_index("leaf") >> (height - 1)) & 1
    pair[0] = mine[...]
    pair[1] = other[...]
    left = pair[on_right]
    right = pair[1 - on_right]
    line = skel[0, height - 1 : height, :]
    weights = dot(left[features:], basis[0, height - 1, :, :skeleton], 1, 1)
    weights += dot(right[features:], basis[0, height - 1, :, skeleton:], 1, 1)
    coords = dot(left[:features], one_hot(line, skeleton), 1, 0)
    coords += dot(right[:features], one_hot(line, skeleton, skeleton), 1, 0)
    node[:features] = coords.astype(BF16)
    node[features:] = weights.astype(BF16)


def entry(lists, line, spot):
    value = lists[line, spot]
    return value & (PACK - 1), value // PACK


def far_sums(line, size, lists, lhs_c, rhs_c, sw, far, begin=0, head=False):
    skeleton = rhs_c.shape[2]
    count = lists[LINES, line]

    def some(start, many):
        results = []
        for index in range(0, many, 2):
            spots = [begin + start + index + half for half in range(2)]
            owns, slots = zip(*[entry(lists, line, spot) for spot in spots])
            blocks = [tile(lhs_c[own], rhs_c[slot], 1, 0) for own, slot in zip(owns, slots)]
            weights = jnp.concatenate([sw[slot, :, size:] for slot in slots], 0)
            part = dot(weights, jnp.concatenate(blocks, 0), 1, 1)
            probes = part.shape[0] // 2
            for half in range(2):
                rows = slice(half * probes, (half + 1) * probes)
                mine = part[rows, half * skeleton : (half + 1) * skeleton]
                mine = mine.astype(BF16).astype(F32)
                results.append((owns[half], jnp.where(spots[half] < count, mine, 0.0)))
        for own, part in results:
            far[own] += part

    if head:
        some(0, FAR_STEP)
    else:
        stepped(count - begin, FAR_STEP, some)


def near_parts(line, start, many, size, lists, lhs_t, rhs, sw):
    count = lists[LINES, line]
    results = []
    for index in range(many):
        spot = start + index
        own, slot = entry(lists, line, spot)
        block = tile(lhs_t[own], rhs[slot], 1, 0)
        part = dot(sw[slot, :, :size], block, 1, 1)
        results.append((own, jnp.where(spot < count, part, 0.0)))
    return results


def near_sums(line, size, lists, lhs_t, rhs, sw, near, done=0):
    def some(start, many):
        for own, part in near_parts(line, start + done, many, size, lists, lhs_t, rhs, sw):
            near[own] += part

    stepped(lists[LINES, line] - done, NEAR_STEP, some)


def stepped(count, many, some):
    half = many // 2
    whole = jnp.maximum(count + half - 1, 0) // many

    def step_of(step, carry):
        some(step * many, many)
        return carry

    lax.fori_loop(0, whole, step_of, 0)

    @pl.when(count > whole * many)
    def _():
        some(whole * many, half)


def first_kernel(
    features, q1, q2, lists_in, lhs_c, _, __, ___, rhs, rhs_c, sw, far, lists, sem
):
    copy = pltpu.make_async_copy(lists_in, lists, sem)
    copy.start()
    build(1, features, q1, q2, rhs, rhs_c, sw)
    far[...] = jnp.zeros_like(far)
    copy.wait()
    far_sums(2, rhs.shape[2], lists, lhs_c, rhs_c, sw, far, head=True)


def other_kernel(
    rel, features, q1, q2, lists_in, lhs_c, after, _, __, ___, ____,
    rhs, rhs_c, sw, far, lists, sem,
):
    copy = pltpu.make_async_copy(lists_in, lists, sem)
    copy.start()
    build(rel, features, q1, q2, rhs, rhs_c, sw)
    copy.wait()
    far_sums(rel + 1, rhs.shape[2], lists, lhs_c, rhs_c, sw, far)


def rest_kernel(size, lists_in, lhs_c, rhs_c, sw, far_in, _, far, lists, sem):
    copy = pltpu.make_async_copy(lists_in, lists, sem)
    copy.start()
    copy.wait()
    far_sums(2, size, lists, lhs_c, rhs_c, sw, far, begin=FAR_STEP)


def mid_kernel(size, lists_in, lhs_t, rhs, sw, near_in, _, near, lists, sem):
    copy = pltpu.make_async_copy(lists_in, lists, sem)
    copy.start()
    copy.wait()
    near_sums(0, size, lists, lhs_t, rhs, sw, near)


def last_kernel(features, levels, *refs):
    nodes, refs = refs[: 2 * levels], refs[2 * levels :]
    upper_basis, subtree_basis, dev_basis, leaf_basis, lists_in, lhs_t, *refs = refs
    rhs, sw, far, near, out, lists, sem = refs
    copy = pltpu.make_async_copy(lists_in, lists, sem)
    copy.start()
    leaves, probes, size = out.shape
    skeleton = nodes[0].shape[1]
    me = lax.axis_index("sub")
    subtree = lax.axis_index("leaf")
    tree = []
    for level in range(levels):
        mine, other = nodes[2 * level], nodes[2 * level + 1]
        block = tile(
            with_norms(mine[:features], True), with_norms(other[:features], False), 0, 0
        )
        tree.append(dot(other[features:], block, 1, 1))
    potential = tree[levels - 1]
    for height in range(levels - 1, 0, -1):
        side = pl.multiple_of(((subtree >> (height - 1)) & 1) * skeleton, skeleton)
        part = upper_basis[0, height - 1, :, pl.ds(side, skeleton)]
        potential = tree[height - 1] + dot(potential.astype(BF16), part, 1, 0)
    spot = pl.multiple_of(me * skeleton, skeleton)
    device = dot(potential.astype(BF16), subtree_basis[0, :, pl.ds(spot, skeleton)], 1, 0)
    spread = dot(device.astype(BF16), dev_basis[0], 1, 0).astype(BF16)
    copy.wait()
    early = near_parts(1, 0, NEAR_STEP // 2, size, lists, lhs_t, rhs, sw)
    for leaf in range(leaves):
        total = spread[:, leaf * skeleton : (leaf + 1) * skeleton].astype(F32) + far[leaf]
        high = total.astype(BF16)
        low = (total - high.astype(F32)).astype(BF16)
        part = dot(jnp.concatenate([high, low], 0), leaf_basis[leaf], 1, 0)
        out[leaf] = near[leaf] + part[:probes] + part[probes:]
    for own, part in early:
        out[own] += part
    near_sums(1, size, lists, lhs_t, rhs, sw, out, NEAR_STEP // 2)


def call(kernel, out_shape, in_specs, micros, *args, scratch=(), aliases=(), out_specs=None):
    return pl.pallas_call(
        kernel,
        out_shape=out_shape,
        in_specs=in_specs,
        out_specs=out_specs or jax.tree.map(lambda _: VMEM, out_shape),
        scratch_shapes=scratch,
        input_output_aliases=dict(aliases),
        compiler_params=pltpu.CompilerParams(vmem_limit_bytes=VMEM_LIMIT),
        cost_estimate=pl.CostEstimate(
            flops=int(micros * 1e9), bytes_accessed=int(micros * 1e6), transcendentals=0
        ),
    )(*args)


def placed(*arrays):
    return [pltpu.with_memory_space_constraint(array, pltpu.HBM) for array in arrays]


def on_device(
    points,
    probe_bits,
    leaf_skel,
    leaf_basis,
    device_skel,
    device_basis,
    subtree_skel,
    subtree_basis,
    upper_skel,
    upper_basis,
    near_pairs,
    near_count,
    far_pairs,
):
    leaves, features, size = points.shape
    probes = probe_bits.shape[1]
    skeleton = leaf_skel.shape[1]
    levels = lax.axis_size("leaf").bit_length() - 1
    cap = near_pairs.shape[1]
    far_cap = far_pairs.shape[1]
    depth = features + AUG
    width = max(-(-3 * cap // 128), -(-3 * far_cap // 128)) * 128
    q1_rows = features + probes + LIST_ROWS + leaves
    slots = 4 * leaves
    pack_rows = leaves * (features + probes) + leaves // 2 * probes
    shape = jax.ShapeDtypeStruct
    rhs_shape = shape((slots, depth, size), BF16)
    rhs_c_shape = shape((slots, depth, skeleton), BF16)
    sw_shape = shape((slots, probes, size + skeleton), BF16)
    near_shape = shape((leaves, probes, size), F32)
    far_shape = shape((leaves, probes, skeleton), F32)
    node_shape = shape((features + probes, skeleton), BF16)
    token_shape = shape(TOKEN, F32)
    line_scratch = [pltpu.SMEM((8, width), jnp.int32), pltpu.SemaphoreType.DMA]

    q1, q2 = call(
        prep_kernel,
        (shape((q1_rows, skeleton), BF16), shape((pack_rows, size), BF16)),
        [HBM] * 7 + [SMEM, HBM],
        4,
        *placed(points, probe_bits, leaf_skel, leaf_basis, device_skel, device_basis),
        *placed(jnp.swapaxes(near_pairs, 1, 2)),
        near_count,
        *placed(jnp.swapaxes(far_pairs, 1, 2)),
        scratch=[
            pltpu.VMEM(points.shape, BF16),
            pltpu.VMEM(probe_bits.shape, jnp.int32),
            pltpu.VMEM(leaf_skel.shape, jnp.int32),
            pltpu.VMEM(leaf_basis.shape, BF16),
            pltpu.VMEM(device_skel.shape, jnp.int32),
            pltpu.VMEM(device_basis.shape[1:], BF16),
            pltpu.VMEM((1, 2, cap), jnp.int32),
            pltpu.VMEM((1, 2, far_cap), jnp.int32),
            pltpu.SemaphoreType.DMA((4 + 4 * CHUNKS,)),
        ],
    )
    q1_one, q1_two, q1_three = (
        flipped(q1, "sub", bits) for bits in (1, 2, 3)
    )
    q2_two = flipped(q2, "sub", 2)
    q2_one = flipped(q2, "sub", 1)

    lhs_t, lhs_c, rhs, rhs_c, sw, near, token = call(
        functools.partial(own_kernel, features),
        (
            shape((leaves, size, depth), BF16),
            shape((leaves, skeleton, depth), BF16),
            rhs_shape,
            rhs_c_shape,
            sw_shape,
            near_shape,
            token_shape,
        ),
        [VMEM] * 2,
        5,
        leaf_skel,
        q2,
    )
    node, lists = call(
        functools.partial(node_kernel, features, probes, cap, far_cap),
        (node_shape, shape((8, width), jnp.int32)),
        [VMEM] * 6 + [ANY],
        2,
        q1,
        q1_one,
        q1_two,
        q1_three,
        subtree_basis,
        subtree_skel,
        token,
        scratch=[pltpu.VMEM((4, q1_rows, skeleton), BF16)],
    )
    nodes = []
    far = after = None
    for height in range(1, levels + 1):
        other = flipped(node, "leaf", 1 << (height - 1))
        nodes += [node, other]
        if height == 1:
            rhs, rhs_c, sw, far = call(
                functools.partial(first_kernel, features),
                (rhs_shape, rhs_c_shape, sw_shape, far_shape),
                [VMEM] * 2 + [ANY, VMEM] + [ANY] * 3,
                5,
                q1_one,
                q2_one,
                lists,
                lhs_c,
                rhs,
                rhs_c,
                sw,
                aliases=((4, 0), (5, 1), (6, 2)),
                scratch=line_scratch,
            )
            after = far
        if height == 2:
            far = call(
                functools.partial(rest_kernel, size),
                far_shape,
                [ANY] + [VMEM] * 4 + [ANY],
                3,
                lists,
                lhs_c,
                rhs_c,
                sw,
                far,
                node,
                aliases=((4, 0),),
                scratch=line_scratch,
            )
            after = far
        if height < levels:
            node = call(
                functools.partial(level_kernel, features, height),
                node_shape,
                [VMEM] * 4 + [ANY],
                1,
                node,
                other,
                upper_basis,
                upper_skel,
                after,
                scratch=[pltpu.VMEM((2, features + probes, skeleton), BF16)],
            )

    near = call(
        functools.partial(mid_kernel, size),
        near_shape,
        [ANY] + [VMEM] * 4 + [ANY],
        5,
        lists,
        lhs_t,
        rhs,
        sw,
        near,
        node,
        aliases=((4, 0),),
        scratch=line_scratch,
    )
    q2_three = flipped(q2_two, "sub", 1)
    for rel, sources in ((2, (q1_two, q2_two)), (3, (q1_three, q2_three))):
        rhs, rhs_c, sw, far = call(
            functools.partial(other_kernel, rel, features),
            (rhs_shape, rhs_c_shape, sw_shape, far_shape),
            [VMEM] * 2 + [ANY, VMEM] + [ANY] * 4 + [VMEM],
            3,
            *sources,
            lists,
            lhs_c,
            node,
            rhs,
            rhs_c,
            sw,
            far,
            aliases=((5, 0), (6, 1), (7, 2), (8, 3)),
            scratch=line_scratch,
        )

    return call(
        functools.partial(last_kernel, features, levels),
        near_shape,
        [VMEM] * (2 * levels + 4) + [ANY] + [VMEM] * 5,
        10,
        *nodes,
        upper_basis,
        subtree_basis,
        device_basis,
        leaf_basis,
        lists,
        lhs_t,
        rhs,
        sw,
        far,
        near,
        scratch=line_scratch,
    )


def solution(mesh):
    return jax.shard_map(
        on_device,
        mesh=mesh,
        in_specs=(
            P(("leaf", "sub"), None, None),
            P(("leaf", "sub"), None, None),
            P(("leaf", "sub"), None),
            P(("leaf", "sub"), None, None),
            P(("leaf", "sub"), None),
            P(("leaf", "sub"), None, None),
            P("leaf", None),
            P("leaf", None, None),
            P("leaf", None, None),
            P("leaf", None, None, None),
            P(("leaf", "sub"), None, None),
            P(("leaf", "sub")),
            P(("leaf", "sub"), None, None),
        ),
        out_specs=P(("leaf", "sub"), None, None),
        check_vma=False,
    )
```

```python
import functools

import jax
import jax.numpy as jnp
from jax import lax
from jax.experimental import pallas as pl
from jax.experimental.pallas import tpu as pltpu
from jax.sharding import PartitionSpec as P


BF16 = jnp.bfloat16
F32 = jnp.float32
AUG = 16
NEAR_STEP = 16
MID_MOST = 3 * NEAR_STEP
OWN_STEP = 8
CHUNKS = 2
FAR_STEP = 32
LIST_ROWS = 16
LINES = 5
PACK = 256
VMEM = pl.BlockSpec(memory_space=pltpu.VMEM)
SMEM = pl.BlockSpec(memory_space=pltpu.SMEM)
ANY = pl.BlockSpec(memory_space=pl.ANY)
HBM = pl.BlockSpec(memory_space=pltpu.HBM)
VMEM_LIMIT = 24 << 20
TOKEN = (8, 128)


def flipped(block, axis, bits):
    count = lax.axis_size(axis)
    return lax.ppermute(block, axis, [(low, low ^ bits) for low in range(count)])


def dot(left, right, left_dim, right_dim):
    return lax.dot_general(
        left, right, (((left_dim,), (right_dim,)), ((), ())), preferred_element_type=F32
    )


def one_hot(columns, rows, start=0):
    spots = lax.broadcasted_iota(jnp.int32, (rows, columns.shape[1]), 0) + start
    return jnp.where(spots == columns, 1.0, 0.0).astype(BF16)


def norm_parts(coords):
    wide = coords.astype(F32)
    norm = jnp.sum(wide * wide, axis=0, keepdims=True) * (-1.0 / coords.shape[0])
    high = norm.astype(BF16).astype(F32)
    rest = norm - high
    middle = rest.astype(BF16).astype(F32)
    return high, middle, rest - middle


def aug_rows(parts, width, norm_first):
    row = lax.broadcasted_iota(jnp.int32, (AUG, width), 0)
    start, ones = (0, 3) if norm_first else (3, 0)
    block = jnp.where((row >= ones) & (row < ones + 3), 1.0, 0.0)
    for index, part in enumerate(parts):
        block = jnp.where(row == start + index, part, block)
    return block.astype(BF16)


def with_norms(coords, norm_first):
    rows = aug_rows(norm_parts(coords), coords.shape[1], norm_first)
    scaled = (coords.astype(F32) * (2.0 / coords.shape[0])).astype(BF16) if norm_first else coords
    return jnp.concatenate([scaled, rows], axis=0)


def tile(left, right, left_dim, right_dim):
    return jnp.exp(dot(left, right, left_dim, right_dim)).astype(BF16)


def parts_of(pack, leaf, leaves, features, probes):
    size = pack.shape[1]
    skeleton = size // 2
    signs = leaves * features + leaf * probes
    weights = leaves * (features + probes) + (leaf // 2) * probes
    side = (leaf % 2) * skeleton
    return (
        pack.at[leaf * features : (leaf + 1) * features],
        pack.at[signs : signs + probes],
        pack.at[weights : weights + probes, side : side + skeleton],
    )


def list_rows(pairs, row, width):
    pick = lax.broadcasted_iota(jnp.int32, (8, 2), 0) == lax.broadcasted_iota(
        jnp.int32, (8, 2), 1
    ) + row
    spread = jnp.where(pick, 1.0, 0.0).astype(BF16)
    rows = dot(spread, pairs.astype(F32).astype(BF16), 1, 0)
    short = width - pairs.shape[1]
    return jnp.concatenate([rows, jnp.zeros((8, short), F32)], axis=1) if short else rows


def prep_kernel(
    points_in, bits_in, skel_in, basis_in, dev_skel_in, dev_basis_in, near_in, near_count, far_in,
    q1, q2, points, bits, leaf_skel, leaf_basis, dev_skel, dev_basis, near, far, sems,
):
    leaves, features, size = points.shape
    probes = bits.shape[1]
    skeleton = leaf_skel.shape[1]
    small = [
        pltpu.make_async_copy(source, target, sems.at[index])
        for index, (source, target) in enumerate(
            ((skel_in, leaf_skel), (dev_skel_in, dev_skel), (near_in, near), (far_in, far))
        )
    ]
    chunk = leaves // CHUNKS
    large = []
    for index in range(CHUNKS):
        rows = pl.ds(index * chunk, chunk)
        columns = pl.ds(index * chunk * skeleton, chunk * skeleton)
        base = 4 + 4 * index
        large.append(
            [
                pltpu.make_async_copy(points_in.at[rows], points.at[rows], sems.at[base]),
                pltpu.make_async_copy(bits_in.at[rows], bits.at[rows], sems.at[base + 1]),
                pltpu.make_async_copy(basis_in.at[rows], leaf_basis.at[rows], sems.at[base + 2]),
                pltpu.make_async_copy(
                    dev_basis_in.at[0, :, columns], dev_basis.at[:, columns], sems.at[base + 3]
                ),
            ]
        )
    for copy in small + [copy for group in large for copy in group]:
        copy.start()
    for copy in small:
        copy.wait()
    lists = list_rows(near[0], 0, skeleton) + list_rows(far[0], 2, skeleton)
    row = lax.broadcasted_iota(jnp.int32, lists.shape, 0)
    lists = jnp.where(row == 4, near_count[0].astype(F32), lists)
    base = features + probes
    q1[base : base + LIST_ROWS] = jnp.concatenate([lists, jnp.zeros_like(lists)], 0).astype(BF16)
    q1[base + LIST_ROWS :] = leaf_skel[...].astype(F32).astype(BF16)
    names = jnp.concatenate(
        [leaf_skel[...].astype(F32), jnp.broadcast_to(dev_skel[...].astype(F32), (8, skeleton))], 0
    ).T
    lane = lax.broadcasted_iota(jnp.int32, (skeleton, size), 1).astype(F32)
    total = jnp.zeros((features + probes, size), F32)
    for first in range(0, leaves, 2):
        if first % chunk == 0:
            for copy in large[first // chunk]:
                copy.wait()
        coords, weights = [], []
        for leaf in (first, first + 1):
            signs = (2 * bits[leaf] - 1).astype(F32).astype(BF16)
            hot = jnp.where(lane == names[:, leaf : leaf + 1], 1.0, 0.0).astype(BF16)
            both = dot(
                jnp.concatenate([points[leaf], signs], 0),
                jnp.concatenate([hot, leaf_basis[leaf]], 0),
                1,
                1,
            ).astype(BF16)
            coords.append(both[:features, :skeleton])
            weights.append(both[features:, skeleton:])
            pack_points, pack_signs, pack_weights = parts_of(q2, leaf, leaves, features, probes)
            pack_points[...] = points[leaf]
            pack_signs[...] = signs
            pack_weights[...] = weights[-1]
        spots = lane + float(first * skeleton)
        hot = jnp.where(spots == names[:, leaves : leaves + 1], 1.0, 0.0).astype(BF16)
        columns = slice(first * skeleton, (first + 2) * skeleton)
        total += dot(
            jnp.concatenate([jnp.concatenate(coords, 1), jnp.concatenate(weights, 1)], 0),
            jnp.concatenate([hot, dev_basis[:, columns]], 0),
            1,
            1,
        )
    q1[:features] = total[:features, :skeleton].astype(BF16)
    q1[features : features + probes] = total[features:, skeleton:].astype(BF16)


def own_kernel(features, leaf_skel, q2, lhs_t, lhs_c, rhs, rhs_c, sw, near, token):
    leaves, probes, size = near.shape
    for leaf in range(leaves):
        points, signs, weights = parts_of(q2, leaf, leaves, features, probes)
        left = with_norms(points[...], True)
        right = with_norms(points[...], False)
        both = dot(
            jnp.concatenate([left, right], 0), one_hot(leaf_skel[leaf : leaf + 1, :], size), 1, 0
        ).astype(BF16)
        rhs[leaf] = right
        lhs_t[leaf] = left.T
        lhs_c[leaf] = both[: features + AUG].T
        rhs_c[leaf] = both[features + AUG :]
        sw[leaf, :, :size] = signs[...]
        sw[leaf, :, size:] = weights[...]

    def step_of(step, carry):
        for index in range(OWN_STEP):
            leaf = step * OWN_STEP + index
            block = tile(lhs_t[leaf], rhs[leaf], 1, 0)
            near[leaf] = dot(sw[leaf, :, :size], block, 1, 1)
        return carry

    lax.fori_loop(0, leaves // OWN_STEP, step_of, 0)
    token[...] = jnp.zeros_like(token)


def node_kernel(
    features, probes, cap, far_cap, mine, one, two, three, basis, skel, token, node, lists, q1
):
    skeleton = mine.shape[1]
    leaves = mine.shape[0] - features - probes - LIST_ROWS
    shift = leaves.bit_length() - 1
    groups = 4
    me = lax.axis_index("sub")
    for rel, ref in enumerate((mine, one, two, three)):
        q1[rel] = ref[...]
    weights = jnp.zeros((probes, skeleton), F32)
    coords = jnp.zeros((features, skeleton), F32)
    for spot in range(groups):
        block = q1[jnp.bitwise_xor(me, spot)]
        span = slice(spot * skeleton, (spot + 1) * skeleton)
        weights += dot(block[features : features + probes], basis[0, :, span], 1, 1)
        coords += dot(block[:features], one_hot(skel[...], skeleton, spot * skeleton), 1, 0)
    node[:features] = coords.astype(BF16)
    node[features:] = weights.astype(BF16)

    base = features + probes
    lane = lax.broadcasted_iota(jnp.int32, (1, skeleton), 1)
    rows = [q1[rel, base : base + LIST_ROWS].astype(F32) for rel in range(groups)]
    whole = [block.astype(jnp.int32) for block in rows]
    segments = []
    for kind, limit in ((0, cap), (2, far_cap)):
        for rel in (None, 0, 1, 2, 3):
            block = whole[0 if rel is None else rel]
            first = block[kind : kind + 1]
            second = block[kind + 1 : kind + 2]
            used = lane < (block[4:5] if kind == 0 else limit)
            owner = second >> shift
            inner = second & (leaves - 1)
            if rel is not None:
                line = rel >> 1 if kind == 0 else 1 + max(rel, 1)
                segments.append((line, inner, rel * leaves + first, used & (owner == me)))
                continue
            apart = jnp.bitwise_xor(owner, me)
            slot = apart * leaves + inner
            if kind == 0:
                segments.append((0, first, slot, used & (apart < 2)))
                segments.append((1, first, slot, used & (apart >= 2)))
            else:
                segments.append((2, first, slot, used & (apart < 2)))
                segments.append((3, first, slot, used & (apart == 2)))
                segments.append((4, first, slot, used & (apart == 3)))
    masks = jnp.concatenate([jnp.where(part[3], 1.0, 0.0) for part in segments], 0)
    masks = jnp.concatenate([masks, jnp.zeros((-len(segments) % 16, skeleton), F32)], 0)
    before = lax.broadcasted_iota(jnp.int32, (skeleton, skeleton), 0) < lax.broadcasted_iota(
        jnp.int32, (skeleton, skeleton), 1
    )
    prefix = dot(masks.astype(BF16), jnp.where(before, 1.0, 0.0).astype(BF16), 1, 0)
    totals = jnp.sum(masks, axis=1, keepdims=True)
    width = lists.shape[1]
    counts = jnp.zeros((1, skeleton), F32)
    for line in range(LINES):
        offset = jnp.zeros((1, 1), F32)
        result = jnp.zeros((8, width), F32)
        for index, part in enumerate(segments):
            if part[0] != line:
                continue
            place = jnp.where(part[3], prefix[index : index + 1] + offset, -1.0)
            offset += totals[index : index + 1]
            spots = lax.broadcasted_iota(jnp.int32, (width, skeleton), 0)
            hot = jnp.where(spots == place.astype(jnp.int32), 1.0, 0.0).astype(BF16)
            values = jnp.concatenate(
                [part[1].astype(F32), part[2].astype(F32), jnp.zeros((6, skeleton), F32)], 0
            ).astype(BF16)
            result += dot(values, hot, 1, 1)
        whole_result = result.astype(jnp.int32)
        lists[line : line + 1] = whole_result[:1] + whole_result[1:2] * PACK
        counts = jnp.where(lane == line, jnp.broadcast_to(offset, (1, skeleton)), counts)
    lists[LINES : LINES + 1, :skeleton] = counts.astype(jnp.int32)
    lists[LINES : LINES + 1, skeleton:] = jnp.zeros((1, width - skeleton), jnp.int32)
    lists[LINES + 1 :] = jnp.zeros((8 - LINES - 1, width), jnp.int32)


def build(rel, features, q1, q2, rhs, rhs_c, sw):
    probes, size = sw.shape[1], rhs.shape[2]
    leaves = rhs.shape[0] // 4
    base = rel * leaves
    skels = q1[q1.shape[0] - leaves :].astype(F32).astype(jnp.int32)
    for leaf in range(leaves):
        points, signs, weights = parts_of(q2, leaf, leaves, features, probes)
        right = with_norms(points[...], False)
        rhs[base + leaf] = right
        rhs_c[base + leaf] = dot(right, one_hot(skels[leaf : leaf + 1], size), 1, 0).astype(BF16)
        sw[base + leaf, :, :size] = signs[...]
        sw[base + leaf, :, size:] = weights[...]


def level_kernel(features, height, mine, other, basis, skel, after, node, pair):
    skeleton = mine.shape[1]
    on_right = (lax.axis_index("leaf") >> (height - 1)) & 1
    pair[0] = mine[...]
    pair[1] = other[...]
    left = pair[on_right]
    right = pair[1 - on_right]
    line = skel[0, height - 1 : height, :]
    weights = dot(left[features:], basis[0, height - 1, :, :skeleton], 1, 1)
    weights += dot(right[features:], basis[0, height - 1, :, skeleton:], 1, 1)
    coords = dot(left[:features], one_hot(line, skeleton), 1, 0)
    coords += dot(right[:features], one_hot(line, skeleton, skeleton), 1, 0)
    node[:features] = coords.astype(BF16)
    node[features:] = weights.astype(BF16)


def entry(lists, line, spot):
    value = lists[line, spot]
    return value & (PACK - 1), value // PACK


def far_sums(line, size, lists, lhs_c, rhs_c, sw, far, begin=0, head=False):
    skeleton = rhs_c.shape[2]
    count = lists[LINES, line]

    def some(start, many):
        results = []
        for index in range(0, many, 2):
            spots = [begin + start + index + half for half in range(2)]
            owns, slots = zip(*[entry(lists, line, spot) for spot in spots])
            blocks = [tile(lhs_c[own], rhs_c[slot], 1, 0) for own, slot in zip(owns, slots)]
            weights = jnp.concatenate([sw[slot, :, size:] for slot in slots], 0)
            part = dot(weights, jnp.concatenate(blocks, 0), 1, 1)
            probes = part.shape[0] // 2
            for half in range(2):
                rows = slice(half * probes, (half + 1) * probes)
                mine = part[rows, half * skeleton : (half + 1) * skeleton]
                mine = mine.astype(BF16).astype(F32)
                results.append((owns[half], jnp.where(spots[half] < count, mine, 0.0)))
        for own, part in results:
            far[own] += part

    if head:
        some(0, FAR_STEP)
    else:
        stepped(count - begin, FAR_STEP, some)


def near_parts(line, start, many, size, lists, lhs_t, rhs, sw):
    count = lists[LINES, line]
    results = []
    for index in range(many):
        spot = start + index
        own, slot = entry(lists, line, spot)
        block = tile(lhs_t[own], rhs[slot], 1, 0)
        part = dot(sw[slot, :, :size], block, 1, 1)
        results.append((own, jnp.where(spot < count, part, 0.0)))
    return results


def near_sums(line, size, lists, lhs_t, rhs, sw, near, done=0, most=None):
    def some(start, many):
        for own, part in near_parts(line, start + done, many, size, lists, lhs_t, rhs, sw):
            near[own] += part

    count = lists[LINES, line]
    if most is not None:
        count = jnp.minimum(count, most)
    stepped(count - done, NEAR_STEP, some)


def stepped(count, many, some):
    half = many // 2
    whole = jnp.maximum(count + half - 1, 0) // many

    def step_of(step, carry):
        some(step * many, many)
        return carry

    lax.fori_loop(0, whole, step_of, 0)

    @pl.when(count > whole * many)
    def _():
        some(whole * many, half)


def first_kernel(
    features, q1, q2, lists_in, lhs_c, _, __, ___, rhs, rhs_c, sw, far, lists, sem
):
    copy = pltpu.make_async_copy(lists_in, lists, sem)
    copy.start()
    build(1, features, q1, q2, rhs, rhs_c, sw)
    far[...] = jnp.zeros_like(far)
    copy.wait()
    far_sums(2, rhs.shape[2], lists, lhs_c, rhs_c, sw, far, head=True)


def other_kernel(
    rel, features, q1, q2, lists_in, lhs_c, after, _, __, ___, ____,
    rhs, rhs_c, sw, far, lists, sem,
):
    copy = pltpu.make_async_copy(lists_in, lists, sem)
    copy.start()
    build(rel, features, q1, q2, rhs, rhs_c, sw)
    copy.wait()
    far_sums(rel + 1, rhs.shape[2], lists, lhs_c, rhs_c, sw, far)


def rest_kernel(size, lists_in, lhs_c, rhs_c, sw, far_in, _, far, lists, sem):
    copy = pltpu.make_async_copy(lists_in, lists, sem)
    copy.start()
    copy.wait()
    far_sums(2, size, lists, lhs_c, rhs_c, sw, far, begin=FAR_STEP)


def mid_kernel(size, lists_in, lhs_t, rhs, sw, near_in, _, near, lists, sem):
    copy = pltpu.make_async_copy(lists_in, lists, sem)
    copy.start()
    copy.wait()
    near_sums(0, size, lists, lhs_t, rhs, sw, near, most=MID_MOST)


def last_kernel(features, levels, *refs):
    nodes, refs = refs[: 2 * levels], refs[2 * levels :]
    upper_basis, subtree_basis, dev_basis, leaf_basis, lists_in, lhs_t, *refs = refs
    rhs, sw, far, near, out, lists, sem = refs
    copy = pltpu.make_async_copy(lists_in, lists, sem)
    copy.start()
    leaves, probes, size = out.shape
    skeleton = nodes[0].shape[1]
    me = lax.axis_index("sub")
    subtree = lax.axis_index("leaf")
    tree = []
    for level in range(levels):
        mine, other = nodes[2 * level], nodes[2 * level + 1]
        block = tile(
            with_norms(mine[:features], True), with_norms(other[:features], False), 0, 0
        )
        tree.append(dot(other[features:], block, 1, 1))
    potential = tree[levels - 1]
    for height in range(levels - 1, 0, -1):
        side = pl.multiple_of(((subtree >> (height - 1)) & 1) * skeleton, skeleton)
        part = upper_basis[0, height - 1, :, pl.ds(side, skeleton)]
        potential = tree[height - 1] + dot(potential.astype(BF16), part, 1, 0)
    spot = pl.multiple_of(me * skeleton, skeleton)
    device = dot(potential.astype(BF16), subtree_basis[0, :, pl.ds(spot, skeleton)], 1, 0)
    spread = dot(device.astype(BF16), dev_basis[0], 1, 0).astype(BF16)
    copy.wait()
    early = near_parts(1, 0, NEAR_STEP // 2, size, lists, lhs_t, rhs, sw)
    for leaf in range(leaves):
        total = spread[:, leaf * skeleton : (leaf + 1) * skeleton].astype(F32) + far[leaf]
        high = total.astype(BF16)
        low = (total - high.astype(F32)).astype(BF16)
        part = dot(jnp.concatenate([high, low], 0), leaf_basis[leaf], 1, 0)
        out[leaf] = near[leaf] + part[:probes] + part[probes:]
    for own, part in early:
        out[own] += part
    near_sums(1, size, lists, lhs_t, rhs, sw, out, NEAR_STEP // 2)
    near_sums(0, size, lists, lhs_t, rhs, sw, out, MID_MOST)


def call(kernel, out_shape, in_specs, micros, *args, scratch=(), aliases=(), out_specs=None):
    return pl.pallas_call(
        kernel,
        out_shape=out_shape,
        in_specs=in_specs,
        out_specs=out_specs or jax.tree.map(lambda _: VMEM, out_shape),
        scratch_shapes=scratch,
        input_output_aliases=dict(aliases),
        compiler_params=pltpu.CompilerParams(vmem_limit_bytes=VMEM_LIMIT),
        cost_estimate=pl.CostEstimate(
            flops=int(micros * 1e9), bytes_accessed=int(micros * 1e6), transcendentals=0
        ),
    )(*args)


def placed(*arrays):
    return [pltpu.with_memory_space_constraint(array, pltpu.HBM) for array in arrays]


def on_device(
    points,
    probe_bits,
    leaf_skel,
    leaf_basis,
    device_skel,
    device_basis,
    subtree_skel,
    subtree_basis,
    upper_skel,
    upper_basis,
    near_pairs,
    near_count,
    far_pairs,
):
    leaves, features, size = points.shape
    probes = probe_bits.shape[1]
    skeleton = leaf_skel.shape[1]
    levels = lax.axis_size("leaf").bit_length() - 1
    cap = near_pairs.shape[1]
    far_cap = far_pairs.shape[1]
    depth = features + AUG
    width = max(-(-3 * cap // 128), -(-3 * far_cap // 128)) * 128
    q1_rows = features + probes + LIST_ROWS + leaves
    slots = 4 * leaves
    pack_rows = leaves * (features + probes) + leaves // 2 * probes
    shape = jax.ShapeDtypeStruct
    rhs_shape = shape((slots, depth, size), BF16)
    rhs_c_shape = shape((slots, depth, skeleton), BF16)
    sw_shape = shape((slots, probes, size + skeleton), BF16)
    near_shape = shape((leaves, probes, size), F32)
    far_shape = shape((leaves, probes, skeleton), F32)
    node_shape = shape((features + probes, skeleton), BF16)
    token_shape = shape(TOKEN, F32)
    line_scratch = [pltpu.SMEM((8, width), jnp.int32), pltpu.SemaphoreType.DMA]

    q1, q2 = call(
        prep_kernel,
        (shape((q1_rows, skeleton), BF16), shape((pack_rows, size), BF16)),
        [HBM] * 7 + [SMEM, HBM],
        4,
        *placed(points, probe_bits, leaf_skel, leaf_basis, device_skel, device_basis),
        *placed(jnp.swapaxes(near_pairs, 1, 2)),
        near_count,
        *placed(jnp.swapaxes(far_pairs, 1, 2)),
        scratch=[
            pltpu.VMEM(points.shape, BF16),
            pltpu.VMEM(probe_bits.shape, jnp.int32),
            pltpu.VMEM(leaf_skel.shape, jnp.int32),
            pltpu.VMEM(leaf_basis.shape, BF16),
            pltpu.VMEM(device_skel.shape, jnp.int32),
            pltpu.VMEM(device_basis.shape[1:], BF16),
            pltpu.VMEM((1, 2, cap), jnp.int32),
            pltpu.VMEM((1, 2, far_cap), jnp.int32),
            pltpu.SemaphoreType.DMA((4 + 4 * CHUNKS,)),
        ],
    )
    q1_one, q1_two, q1_three = (
        flipped(q1, "sub", bits) for bits in (1, 2, 3)
    )
    q2_two = flipped(q2, "sub", 2)
    q2_one = flipped(q2, "sub", 1)

    lhs_t, lhs_c, rhs, rhs_c, sw, near, token = call(
        functools.partial(own_kernel, features),
        (
            shape((leaves, size, depth), BF16),
            shape((leaves, skeleton, depth), BF16),
            rhs_shape,
            rhs_c_shape,
            sw_shape,
            near_shape,
            token_shape,
        ),
        [VMEM] * 2,
        5,
        leaf_skel,
        q2,
    )
    node, lists = call(
        functools.partial(node_kernel, features, probes, cap, far_cap),
        (node_shape, shape((8, width), jnp.int32)),
        [VMEM] * 6 + [ANY],
        2,
        q1,
        q1_one,
        q1_two,
        q1_three,
        subtree_basis,
        subtree_skel,
        token,
        scratch=[pltpu.VMEM((4, q1_rows, skeleton), BF16)],
    )
    nodes = []
    far = after = None
    for height in range(1, levels + 1):
        other = flipped(node, "leaf", 1 << (height - 1))
        nodes += [node, other]
        if height == 1:
            rhs, rhs_c, sw, far = call(
                functools.partial(first_kernel, features),
                (rhs_shape, rhs_c_shape, sw_shape, far_shape),
                [VMEM] * 2 + [ANY, VMEM] + [ANY] * 3,
                5,
                q1_one,
                q2_one,
                lists,
                lhs_c,
                rhs,
                rhs_c,
                sw,
                aliases=((4, 0), (5, 1), (6, 2)),
                scratch=line_scratch,
            )
            after = far
        if height == 2:
            far = call(
                functools.partial(rest_kernel, size),
                far_shape,
                [ANY] + [VMEM] * 4 + [ANY],
                3,
                lists,
                lhs_c,
                rhs_c,
                sw,
                far,
                node,
                aliases=((4, 0),),
                scratch=line_scratch,
            )
            after = far
        if height < levels:
            node = call(
                functools.partial(level_kernel, features, height),
                node_shape,
                [VMEM] * 4 + [ANY],
                1,
                node,
                other,
                upper_basis,
                upper_skel,
                after,
                scratch=[pltpu.VMEM((2, features + probes, skeleton), BF16)],
            )

    near = call(
        functools.partial(mid_kernel, size),
        near_shape,
        [ANY] + [VMEM] * 4 + [ANY],
        5,
        lists,
        lhs_t,
        rhs,
        sw,
        near,
        node,
        aliases=((4, 0),),
        scratch=line_scratch,
    )
    q2_three = flipped(q2_two, "sub", 1)
    for rel, sources in ((2, (q1_two, q2_two)), (3, (q1_three, q2_three))):
        rhs, rhs_c, sw, far = call(
            functools.partial(other_kernel, rel, features),
            (rhs_shape, rhs_c_shape, sw_shape, far_shape),
            [VMEM] * 2 + [ANY, VMEM] + [ANY] * 4 + [VMEM],
            3,
            *sources,
            lists,
            lhs_c,
            node,
            rhs,
            rhs_c,
            sw,
            far,
            aliases=((5, 0), (6, 1), (7, 2), (8, 3)),
            scratch=line_scratch,
        )

    return call(
        functools.partial(last_kernel, features, levels),
        near_shape,
        [VMEM] * (2 * levels + 4) + [ANY] + [VMEM] * 5,
        10,
        *nodes,
        upper_basis,
        subtree_basis,
        device_basis,
        leaf_basis,
        lists,
        lhs_t,
        rhs,
        sw,
        far,
        near,
        scratch=line_scratch,
    )


def solution(mesh):
    return jax.shard_map(
        on_device,
        mesh=mesh,
        in_specs=(
            P(("leaf", "sub"), None, None),
            P(("leaf", "sub"), None, None),
            P(("leaf", "sub"), None),
            P(("leaf", "sub"), None, None),
            P(("leaf", "sub"), None),
            P(("leaf", "sub"), None, None),
            P("leaf", None),
            P("leaf", None, None),
            P("leaf", None, None),
            P("leaf", None, None, None),
            P(("leaf", "sub"), None, None),
            P(("leaf", "sub")),
            P(("leaf", "sub"), None, None),
        ),
        out_specs=P(("leaf", "sub"), None, None),
        check_vma=False,
    )
```
